256 devices in a mesh: elem: 16 (over z_lo, y, core), mode: 16 (over z_hi, x).
Axes of the slice: x: 4, y: 4, z: 8 (z_hi: 4, z_lo: 2; z = z_hi * 2 + z_lo), core: 2. Of those that a mesh axis runs over, the one named last changes fastest.
Arguments:
- coeff: float32 [64, 256, 2048], P(None, 'mode', 'elem'), as said below
- vel_axial: bfloat16 [64, 256, 2048], P('mode', None, 'elem'), may hold values from -3 to 3
- vel_radial: bfloat16 [64, 256, 2048], P('mode', None, 'elem'), may hold values from -3 to 3
- swirl_rate: bfloat16 [64, 256, 2048], P('mode', None, 'elem'), may hold values from -3 to 3
- col_width: float32 [128], P('elem'), may hold values from 0.5 to 2
- row_height: float32 [16], replicated, may hold values from 0.5 to 2
- stiffness: float32 [64, 64], replicated
- stiff_elem: float32 [2048], P('elem'), may hold values from 0.5 to 4
- mass: float32 [64, 2048], P(None, 'elem'), may hold values from 0.25 to 1
- azim_weight: float32 [64, 2048], P(None, 'elem'), may hold values from 0.5 to 8
- wall_flag: int32 [128], P('elem'), may hold values 0 or 1
- transfer: float32 [128], P('elem'), may hold values from 0.5 to 4
Outputs:
- solution: float32 [64, 256, 2048], P(None, 'mode', 'elem')
The draws below stay inside these ranges and needn't reach their ends.
Inputs may be any that keep to these rules, and one draw needn't show every extreme that they name: `coeff`: every grid point that neighbouring elements share has the same coefficients in each of them.
All inputs are finite; a program needn't handle non-finite values. No bound on the sum of `wall_flag` on one device may be relied on, other than what follows from the above.
Results may differ from the reference program's by a relative error of at most 0.0003.
Values sent between devices are 32-bit elements; how exact they have to be, the bound alone decides.
A program may use at most 64 MiB of HBM per device.

```python
import math
import jax
import jax.numpy as jnp
import numpy as np
from jax import lax

NODE_SIDE = 8
NODES = 64
PLANES = 256
EY = 16
EXT = 128
ELEMS = 2048
SWEEPS = 3


def draw_coeff(key, part):
    side_count = NODE_SIDE
    grid_x = (side_count - 1) * EXT + 1
    grid_y = (side_count - 1) * EY + 1
    values = jax.random.normal(key, (PLANES, grid_y, grid_x), jnp.float32)
    coeff_idx = jnp.arange(PLANES, dtype=jnp.int32)
    wavenum = ((coeff_idx + 1) // 2).astype(jnp.float32)
    values = values / (1.0 + wavenum / 4.0)[:, None, None]
    local_idx = jnp.arange(side_count, dtype=jnp.int32)
    y_index = (side_count - 1) * jnp.arange(EY, dtype=jnp.int32)[None, None, None, :] + local_idx[:, None, None, None]
    x_index = (side_count - 1) * jnp.arange(EXT, dtype=jnp.int32)[None, None, :, None] + local_idx[None, :, None, None]
    picked = values[:, y_index, x_index]
    return jnp.transpose(picked, (1, 2, 0, 3, 4)).reshape(side_count * side_count, PLANES, EXT * EY)


def draw_stiffness(key, part):
    size_all = NODE_SIDE * NODE_SIDE
    key_off = jax.random.fold_in(key, 11)
    key_diag = jax.random.fold_in(key, 23)
    raw_off = jax.random.uniform(key_off, (size_all, size_all), jnp.float32, -0.1, 0.1)
    offdiag = 0.5 * (raw_off + raw_off.T)
    eye_mask = jnp.eye(size_all, dtype=jnp.float32)
    diag_vals = jax.random.uniform(key_diag, (size_all,), jnp.float32, 6.5, 8.5)
    return offdiag * (1.0 - eye_mask) + eye_mask * diag_vals[None, :]


def touch_ends(result, rng, smallest, largest):
    longest = result.shape.index(max(result.shape))
    spots = []
    for shift in (0, 1):
        where = [jax.random.randint(jax.random.fold_in(rng, axis), (), 0, length) for axis, length in enumerate(result.shape)]
        where[longest] = (where[longest] + shift) % result.shape[longest]
        spots.append(tuple(where))
    return result.at[spots[0]].set(smallest).at[spots[1]].set(largest)


def steps_of(stream_key, dims, shards, least, top_value):
    factor_of, own = 1.0, jax.random.fold_in(stream_key, 6)
    for dim, parts in shards:
        steps = jnp.exp(jax.random.uniform(jax.random.fold_in(own, dim), (parts,), jnp.float32, least / len(shards), top_value / len(shards)))
        factor_of = factor_of * jnp.repeat(steps, dims[dim] // parts).reshape([-1 if axis == dim else 1 for axis in range(len(dims))])
    return factor_of


def centred(rng, dims, scale, bound, shards=(), held_as=jnp.bfloat16):
    entries = jax.random.normal(rng, dims, jnp.float32) * scale
    if len(shards) > 0:
        entries = steps_of(rng, dims, shards, -0.22, 0.18) * entries
    return jnp.clip(entries, min=-bound, max=bound).astype(held_as)


def setup_inputs(seed: int = 0) -> dict:
    key_list = jax.random.split(jax.random.key(seed), 13)
    return {
        "coeff": draw_coeff(jax.random.fold_in(key_list[12], 71), 0),
        "vel_axial": centred(key_list[1], (NODES, PLANES, ELEMS), 0.5, 3.0, ((0, 16), (2, 16))),
        "vel_radial": centred(key_list[2], (NODES, PLANES, ELEMS), 0.5, 3.0, ((0, 16), (2, 16))),
        "swirl_rate": centred(key_list[3], (NODES, PLANES, ELEMS), 0.5, 3.0, ((0, 16), (2, 16))),
        "col_width": jnp.clip(jnp.exp(math.log(2.0) - 1.3862944 * jax.random.uniform(key_list[4], (EXT,), jnp.float32) ** steps_of(key_list[4], (EXT,), ((0, 16),), -0.2, 0.2)), 0.5, 2.0),
        "row_height": jnp.clip(jnp.exp(jax.random.uniform(key_list[5], (EY,), jnp.float32, math.log(0.5), math.log(2.0))), 0.5, 2.0),
        "stiffness": draw_stiffness(jax.random.fold_in(key_list[12], 71), 0),
        "stiff_elem": jnp.clip(jnp.exp(math.log(4.0) - 2.0794415 * jax.random.uniform(key_list[7], (ELEMS,), jnp.float32) ** steps_of(key_list[7], (ELEMS,), ((0, 16),), -0.2, 0.2)), 0.5, 4.0),
        "mass": jnp.clip(jnp.exp(math.log(1.0) - 1.3862944 * jax.random.uniform(key_list[8], (NODES, ELEMS), jnp.float32) ** steps_of(key_list[8], (NODES, ELEMS), ((1, 16),), -0.2, 0.2)), 0.25, 1.0),
        "azim_weight": jnp.clip(jnp.exp(math.log(8.0) - 2.7725887 * jax.random.uniform(key_list[9], (NODES, ELEMS), jnp.float32) ** steps_of(key_list[9], (NODES, ELEMS), ((1, 16),), -0.2, 0.2)), 0.5, 8.0),
        "wall_flag": touch_ends((jax.random.randint(key_list[10], (EXT,), 0, 2) < 1).astype(jnp.int32), jax.random.fold_in(key_list[10], 1), 0, 1),
        "transfer": jnp.clip(jnp.exp(math.log(4.0) - 2.0794415 * jax.random.uniform(key_list[11], (EXT,), jnp.float32) ** steps_of(key_list[11], (EXT,), ((0, 16),), -0.2, 0.2)), 0.5, 4.0),
    }


FULL_PREC = lax.Precision.HIGHEST
INV_STEP = 2.0
RELAX = 0.8


def cheb_matrix(side_count):
    points = np.cos(np.pi * np.arange(side_count) / (side_count - 1))
    sign_weights = np.ones(side_count)
    sign_weights[0] = 2.0
    sign_weights[side_count - 1] = 2.0
    sign_weights = sign_weights * (-1.0) ** np.arange(side_count)
    diff_table = np.zeros((side_count, side_count))
    for row_index in range(side_count):
        for col_index in range(side_count):
            if row_index != col_index:
                diff_table[row_index, col_index] = sign_weights[row_index] / sign_weights[col_index] / (points[row_index] - points[col_index])
        diff_table[row_index, row_index] = -np.sum(diff_table[row_index])
    return diff_table


def node_operators(side_count):
    diff_table = cheb_matrix(side_count)
    identity = np.eye(side_count)
    axial_op = jnp.asarray(np.kron(identity, diff_table), dtype=jnp.float32)
    radial_op = jnp.asarray(np.kron(diff_table, identity), dtype=jnp.float32)
    return axial_op, radial_op


def wave_numbers(first_row, row_count):
    coeff_idx = first_row + jnp.arange(row_count, dtype=jnp.int32)
    return coeff_idx, (coeff_idx + 1) // 2


def fourier_tables(plane_count):
    coeff_idx, wavenum = wave_numbers(0, plane_count)
    plane_idx = jnp.arange(plane_count, dtype=jnp.int32)
    phase_int = (wavenum[:, None] * plane_idx[None, :]) % plane_count
    angles = (2.0 * math.pi / plane_count) * phase_int.astype(jnp.float32)
    cosine = jnp.cos(angles)
    sine_vals = jnp.sin(angles)
    is_sine = ((coeff_idx % 2 == 0) & (coeff_idx > 0))[:, None]
    wave_col = wavenum.astype(jnp.float32)[:, None]
    basis_tab = jnp.where(is_sine, sine_vals, cosine)
    slope_tab = jnp.where(is_sine, wave_col * cosine, -wave_col * sine_vals)
    norm_fac = jnp.where((coeff_idx == 0) | (coeff_idx == plane_count - 1), jnp.float32(1.0), jnp.float32(2.0)) / plane_count
    forward_tab = basis_tab * norm_fac[:, None]
    return basis_tab, slope_tab, forward_tab


def wave_factor(first_row, row_count, plane_count):
    wavenum = wave_numbers(first_row, row_count)[1]
    return (2.0 * wavenum.astype(jnp.float32) / plane_count) ** 2


def apply_nodes(node_op, field):
    shape_all = field.shape
    flat = field.reshape(shape_all[0], -1)
    return jnp.dot(node_op, flat, precision=FULL_PREC, preferred_element_type=jnp.float32).reshape(shape_all)


def to_phys(panel, dft_table):
    return jnp.einsum('nqe,qp->npe', panel, dft_table, precision=FULL_PREC)


def wall_terms(wall_flag, transfer, rows_here, side_count):
    flag_rate = jnp.repeat(wall_flag.astype(jnp.float32) * transfer, rows_here)
    bottom = (jnp.arange(flag_rate.shape[0], dtype=jnp.int32) % rows_here) == 0
    node_low = jnp.arange(side_count * side_count, dtype=jnp.int32) < side_count
    return jnp.where(node_low[:, None] & bottom[None, :], flag_rate[None, :], jnp.float32(0.0))


def helm_apply(field, stiffness, stiff_elem, lam):
    spread = apply_nodes(stiffness, field)
    return stiff_elem[None, None, :] * spread + lam * field


def assemble_edges(values, cols_here, rows_here, side_count, neighbour):
    width = values.shape[1]
    last = side_count - 1
    grid = values.reshape(side_count, side_count, width, cols_here, rows_here)
    left_edge = grid[:, 0]
    right_edge = grid[:, last]
    outer_left, outer_right = neighbour(left_edge[:, :, 0], right_edge[:, :, cols_here - 1])
    from_left = jnp.concatenate([outer_left[:, :, None], right_edge[:, :, :-1]], axis=2)
    from_right = jnp.concatenate([left_edge[:, :, 1:], outer_right[:, :, None]], axis=2)
    grid = jnp.concatenate([(left_edge + from_left)[:, None], grid[:, 1:last], (right_edge + from_right)[:, None]], axis=1)
    lower = grid[0]
    upper = grid[last]
    zero_row = jnp.zeros_like(lower[..., :1])
    below = jnp.concatenate([zero_row, upper[..., :-1]], axis=-1)
    above = jnp.concatenate([lower[..., 1:], zero_row], axis=-1)
    grid = jnp.concatenate([(lower + below)[None], grid[1:last], (upper + above)[None]], axis=0)
    return grid.reshape(values.shape)


def closed_edges(first_left, last_right):
    return jnp.zeros_like(last_right), jnp.zeros_like(first_left)


def reference(coeff, vel_axial, vel_radial, swirl_rate, col_width, row_height, stiffness, stiff_elem, mass, azim_weight, wall_flag, transfer):
    axial_op, radial_op = node_operators(NODE_SIDE)
    basis_tab, slope_tab, forward_tab = fourier_tables(PLANES)
    axial_scale = jnp.repeat(2.0 / col_width, EY)
    radial_scale = jnp.tile(2.0 / row_height, EXT)
    grad_x = apply_nodes(axial_op, coeff) * axial_scale[None, None, :]
    grad_y = apply_nodes(radial_op, coeff) * radial_scale[None, None, :]

    def advect_block(pieces):
        block_x, block_y, block_c, speed_a, speed_r, speed_s = pieces
        phys_x = to_phys(block_x, basis_tab)
        phys_y = to_phys(block_y, basis_tab)
        phys_t = to_phys(block_c, slope_tab)
        advect = speed_a.astype(jnp.float32) * phys_x + speed_r.astype(jnp.float32) * phys_y + speed_s.astype(jnp.float32) * phys_t
        return jnp.einsum('npe,qp->nqe', advect, forward_tab, precision=FULL_PREC)

    shaped = tuple(item.reshape(NODE_SIDE, NODE_SIDE, PLANES, ELEMS) for item in (grad_x, grad_y, coeff, vel_axial, vel_radial, swirl_rate))
    adv_hat = lax.map(advect_block, shaped).reshape(NODES, PLANES, ELEMS)

    wave_fac = wave_factor(0, PLANES, PLANES)
    wall = wall_terms(wall_flag, transfer, EY, NODE_SIDE)
    lam = (INV_STEP + wave_fac[None, :, None] * azim_weight[:, None, :]) * mass[:, None, :] + wall[:, None, :]
    diag_loc = (jnp.diagonal(stiffness)[:, None] * stiff_elem[None, :])[:, None, :] + lam
    assembled_diag = assemble_edges(diag_loc, EXT, EY, NODE_SIDE, closed_edges)
    rhs_loc = mass[:, None, :] * (INV_STEP * coeff - adv_hat)
    assembled_rhs = assemble_edges(rhs_loc, EXT, EY, NODE_SIDE, closed_edges)
    field = coeff
    for sweep_idx in range(SWEEPS):
        applied = helm_apply(field, stiffness, stiff_elem, lam)
        resid = assembled_rhs - assemble_edges(applied, EXT, EY, NODE_SIDE, closed_edges)
        field = field + RELAX * resid / assembled_diag
    return field
```

```python
import functools

import jax
import jax.numpy as jnp
import ml_dtypes
import numpy as np
from jax import lax
from jax.experimental import pallas as pl
from jax.experimental.pallas import tpu as pltpu
from jax.sharding import PartitionSpec as P

MESH = pl.DeviceIdType.MESH
SIDE = 8
NODES = 64
SWEEPS = 3
INV_STEP = 2.0
RELAX = 0.8
RING = 4
F32 = jnp.float32
BF16 = jnp.bfloat16


def cheb_matrix(side_count):
    points = np.cos(np.pi * np.arange(side_count) / (side_count - 1))
    weights = np.ones(side_count)
    weights[0] = weights[-1] = 2.0
    weights = weights * (-1.0) ** np.arange(side_count)
    table = np.zeros((side_count, side_count))
    for row in range(side_count):
        for col in range(side_count):
            if row != col:
                table[row, col] = weights[row] / weights[col] / (points[row] - points[col])
        table[row, row] = -np.sum(table[row])
    return table


def split_table(table):
    high = table.astype(np.float32).astype(ml_dtypes.bfloat16)
    low = (table - high.astype(np.float64)).astype(np.float32).astype(ml_dtypes.bfloat16)
    return [high, low]


def fourier_tables(planes):
    q = np.arange(planes)
    k = (q + 1) // 2
    angle = 2.0 * np.pi / planes * ((k[:, None] * np.arange(planes)[None, :]) % planes)
    sine = ((q % 2 == 0) & (q > 0))[:, None]
    wave = k[:, None].astype(np.float64)
    basis = np.where(sine, np.sin(angle), np.cos(angle))
    slope = np.where(sine, wave * np.cos(angle), -wave * np.sin(angle))
    norm = np.where((q == 0) | (q == planes - 1), 1.0, 2.0) / planes
    forward = basis * norm[:, None]
    return np.stack(split_table(slope.T) + split_table(basis.T) + split_table(forward))


def split(value):
    high = value.astype(BF16)
    return high, (value - high.astype(F32)).astype(BF16)


def dot3(tab_high, tab_low, value):
    high, low = split(value)
    total = jnp.dot(tab_high, high, preferred_element_type=F32)
    total += jnp.dot(tab_high, low, preferred_element_type=F32)
    return total + jnp.dot(tab_low, high, preferred_element_type=F32)


def kernel(
    modes, coeff, vel_t, vel_y, vel_x, tables, col_width, row_height, stiff, stiff_elem, mass, azim,
    wall_flag, transfer, out,
    vel, tab, grad_y, zbuf, xbuf, hat, adv, fld, lam, rate, load, res, hsend, hrecv,
    local_sem, zs, zr, xs, xr, bs, br, hs, hr,
):
    s, m = lax.axis_index("elem"), lax.axis_index("mode")
    elems = lax.axis_size("elem")
    z, x = m // RING, m % RING
    cheb = cheb_matrix(SIDE)

    fetches = [
        pltpu.make_async_copy(src, dst, local_sem.at[i])
        for i, (src, dst) in enumerate(
            [(vel_t, vel.at[0]), (vel_y, vel.at[1]), (vel_x, vel.at[2]), (tables, tab)]
        )
    ]
    for fetch in fetches:
        fetch.start()

    left, right = lax.rem(s + elems - 1, elems), lax.rem(s + 1, elems)
    barrier = pltpu.get_barrier_semaphore()
    for step in range(1, RING):
        pl.semaphore_signal(
            barrier, inc=1, device_id={"mode": (z + step) % RING * RING + x}, device_id_type=MESH
        )
        pl.semaphore_signal(
            barrier, inc=1, device_id={"mode": z * RING + (x + step) % RING}, device_id_type=MESH
        )
    for other in (left, right):
        pl.semaphore_signal(barrier, inc=1, device_id={"elem": other}, device_id_type=MESH)

    lane = lax.broadcasted_iota(jnp.int32, (1, 128), 1)
    col, row = lane // 16, lane % 16
    width = jnp.zeros((1, 128), F32)
    flow = jnp.zeros((1, 128), F32)
    for a in range(8):
        width = jnp.where(col == a, col_width[a], width)
        flow = jnp.where(col == a, wall_flag[a].astype(F32) * transfer[a], flow)
    flow = jnp.where(row == 0, flow, 0.0)
    height = jnp.zeros((1, 128), F32)
    for b in range(16):
        height = jnp.where(row == b, row_height[b], height)
    scale_x = 2.0 / width
    scale_y = 2.0 / height

    @pl.loop(0, SIDE)
    def _(i):
        start = pl.multiple_of(i * 16, 16)
        cells = [coeff[pl.ds(start + j * 128, 16), :] for j in range(SIDE)]
        for j in range(SIDE):
            total = cheb[j, 0] * cells[0]
            for k in range(1, SIDE):
                total += cheb[j, k] * cells[k]
            grad_y[pl.ds(start + j * 128, 16), :] = total * scale_y

    pl.semaphore_wait(barrier, 2 * (RING - 1) + 2)

    own_row = x // 2
    rows = (1 - own_row, own_row)
    zcopy = {}

    def start_z(d, rr):
        target = (z + d) % RING
        block = pl.ds(pl.multiple_of((target * 2 + rows[rr]) * 128, 128), 128)
        for kind, src in ((0, coeff), (1, grad_y)):
            copy = pltpu.make_async_remote_copy(
                src_ref=src.at[block],
                dst_ref=zbuf.at[z, rows[rr], kind],
                send_sem=zs.at[d - 1, rr, kind],
                recv_sem=zr.at[d - 1, rr, kind],
                device_id={"mode": target * RING + x},
                device_id_type=MESH,
            )
            copy.start()
            zcopy[d, rr, kind] = copy

    for rr in range(2):
        start_z(1, rr)
        start_z(3, rr)
    for rr in range(2):
        start_z(2, rr)

    partner = {1: x + 1 - 2 * (x % 2), 2: (x + 2) % RING, 3: RING - 1 - x}
    xcopy = {}

    def pass_on(k, source, rr):
        line = rows[rr]
        cells = [zbuf[source, line, 0, 16 * i : 16 * i + 16, :] for i in range(SIDE)]
        for i in range(SIDE):
            total = cheb[i, 0] * cells[0]
            for j in range(1, SIDE):
                total += cheb[i, j] * cells[j]
            zbuf[source, line, 2, 16 * i : 16 * i + 16, :] = total * scale_x
        for mask in (2, 3) if rr == 0 else (1,):
            target = partner[mask]
            copy = pltpu.make_async_remote_copy(
                src_ref=zbuf.at[source, line, :, pl.ds(pl.multiple_of(target % 2 * 64, 64), 64)],
                dst_ref=xbuf.at[source * RING + x],
                send_sem=xs.at[k, mask - 1],
                recv_sem=xr.at[k, mask - 1],
                device_id={"mode": z * RING + target},
                device_id_type=MESH,
            )
            copy.start()
            xcopy[k, mask] = copy
        if rr == 1:
            xbuf[source * RING + x] = zbuf[
                source, line, :, pl.ds(pl.multiple_of(x % 2 * 64, 64), 64), :
            ]

    for rr in range(2):
        block = pl.ds(pl.multiple_of((z * 2 + rows[rr]) * 128, 128), 128)
        zbuf[z, rows[rr], 0] = coeff[block, :]
        zbuf[z, rows[rr], 1] = grad_y[block, :]
        pass_on(0, z, rr)

    elem_scale = stiff_elem[...]
    ones = mass[...]
    weights = azim[...]
    node = lax.broadcasted_iota(jnp.int32, (NODES, 128), 0)
    wall = jnp.where(node < SIDE, jnp.broadcast_to(flow, (NODES, 128)), 0.0)
    stiffness = stiff[...]
    on_diag = lax.broadcasted_iota(jnp.int32, (NODES, NODES), 0) == lax.broadcasted_iota(
        jnp.int32, (NODES, NODES), 1
    )
    stiff_diag = jnp.sum(jnp.where(on_diag, stiffness, 0.0), axis=1, keepdims=True) * elem_scale
    stiff_high, stiff_low = split(stiffness)

    def helmholtz(pair):
        both = jnp.concatenate([fld[2 * pair], fld[2 * pair + 1]], axis=1)
        spread = dot3(stiff_high, stiff_low, both)
        return [
            elem_scale * spread[:, 128 * h : 128 * h + 128] + lam[2 * pair + h] * fld[2 * pair + h]
            for h in range(2)
        ]

    for q in range(modes):
        wave = ((m * modes + q + 1) // 2).astype(F32) * (2.0 / (modes * RING * RING))
        lam[q] = (INV_STEP + (wave * wave) * weights) * ones + wall
        rate[q] = stiff_diag + lam[q]
        fld[q] = coeff[pl.ds(q, NODES, stride=modes), :]

    def send_edges(values, turn):
        for g in range(2):
            first = jnp.zeros((SIDE, 128), F32)
            last = jnp.zeros((SIDE, 128), F32)
            for k in range(8):
                q = 8 * g + k
                low = values[q, pl.ds(0, SIDE, stride=SIDE), :]
                high = values[q, pl.ds(SIDE - 1, SIDE, stride=SIDE), :]
                if k > 0:
                    low = pltpu.roll(low, 16 * k, 1)
                if k < 7:
                    high = pltpu.roll(high, 16 * k + 16, 1)
                first = jnp.where(col == k, low, first)
                last = jnp.where(col == k, high, last)
            hsend[turn, 0, g] = first
            hsend[turn, 1, g] = last
        copies = []
        for side, other in ((0, left), (1, right)):
            copy = pltpu.make_async_remote_copy(
                src_ref=hsend.at[turn, side],
                dst_ref=hrecv.at[turn, 1 - side],
                send_sem=hs.at[turn, side],
                recv_sem=hr.at[turn, 1 - side],
                device_id={"elem": other},
                device_id_type=MESH,
            )
            copy.start()
            copies.append(copy)
        return copies

    has_left = (s > 0).astype(F32)
    has_right = (s < elems - 1).astype(F32)

    def assemble(values, turn, copies):
        for copy in copies:
            copy.wait()
        for g in range(2):
            from_left = hrecv[turn, 0, g] * has_left
            from_right = hrecv[turn, 1, g] * has_right
            for k in range(8):
                q = 8 * g + k
                low = values[q, pl.ds(0, SIDE, stride=SIDE), :]
                high = values[q, pl.ds(SIDE - 1, SIDE, stride=SIDE), :]
                near = pltpu.roll(from_left, 128 - 16 * k, 1) if k > 0 else from_left
                far = pltpu.roll(from_right, 112 - 16 * k, 1) if k < 7 else from_right
                values[q, pl.ds(0, SIDE, stride=SIDE), :] = low + jnp.where(
                    col == 0, near, pltpu.roll(high, 16, 1)
                )
                values[q, pl.ds(SIDE - 1, SIDE, stride=SIDE), :] = high + jnp.where(
                    col == 7, far, pltpu.roll(low, 112, 1)
                )
                lower = values[q, 0:SIDE, :]
                upper = values[q, NODES - SIDE : NODES, :]
                values[q, 0:SIDE, :] = lower + jnp.where(row > 0, pltpu.roll(upper, 1, 1), 0.0)
                values[q, NODES - SIDE : NODES, :] = upper + jnp.where(
                    row < 15, pltpu.roll(lower, 127, 1), 0.0
                )

    diag_copies = send_edges(rate, 0)
    for pair in range(modes // 2):
        for h, applied in enumerate(helmholtz(pair)):
            q = 2 * pair + h
            load[q] = INV_STEP * ones * fld[q]
            res[q] = load[q] - applied
    assemble(rate, 0, diag_copies)
    for q in range(modes):
        rate[q] = RELAX / rate[q]

    for k, d in ((1, 1), (2, 3), (3, 2)):
        for rr in range(2):
            for kind in range(2):
                zcopy[d, rr, kind].wait_recv()
            pass_on(k, (z - d + RING) % RING, rr)

    for fetch in fetches:
        fetch.wait()
    for copy in xcopy.values():
        copy.wait_recv()

    for pair in range(2):
        advect = None
        for kind in range(3):
            pieces = [
                xbuf[:, kind, 32 * pair + 16 * h : 32 * pair + 16 * h + 16, :].reshape(-1, 128)
                for h in range(2)
            ]
            which = 0 if kind == 0 else 2
            phys = dot3(tab[which], tab[which + 1], jnp.concatenate(pieces, axis=1))
            speed = jnp.concatenate([vel[kind, 2 * pair], vel[kind, 2 * pair + 1]], axis=1)
            term = speed.astype(F32) * phys
            advect = term if advect is None else advect + term
        back = dot3(tab[4], tab[5], advect)
        for h in range(2):
            for t in range(RING * RING):
                at = t * 64 + (2 * pair + h) * 16
                hat[at : at + 16, :] = back[16 * t : 16 * t + 16, 128 * h : 128 * h + 128]

    mine = pl.ds(pl.multiple_of(m * 64, 64), 64)
    bcopy = []
    for d in range(1, RING * RING):
        target = (m + d) % (RING * RING)
        copy = pltpu.make_async_remote_copy(
            src_ref=hat.at[pl.ds(pl.multiple_of(target * 64, 64), 64)],
            dst_ref=adv.at[mine],
            send_sem=bs.at[d - 1],
            recv_sem=br.at[d - 1],
            device_id={"mode": target},
            device_id_type=MESH,
        )
        copy.start()
        bcopy.append(copy)
    adv[mine, :] = hat[mine, :]
    for copy in bcopy:
        copy.wait_recv()

    for q in range(modes):
        push = ones * adv[pl.ds(q, NODES, stride=modes), :]
        load[q] = load[q] - push
        res[q] = res[q] - push

    for sweep in range(SWEEPS):
        assemble(res, sweep + 1, send_edges(res, sweep + 1))
        if sweep < SWEEPS - 1:
            for q in range(modes):
                fld[q] = fld[q] + rate[q] * res[q]
            for pair in range(modes // 2):
                for h, applied in enumerate(helmholtz(pair)):
                    res[2 * pair + h] = load[2 * pair + h] - applied
        else:
            for q in range(modes):
                out[pl.ds(q, NODES, stride=modes), :] = fld[q] + rate[q] * res[q]

    for copies in (zcopy, xcopy):
        for copy in copies.values():
            copy.wait_send()
    for copy in bcopy:
        copy.wait_send()


def local(
    tables, coeff, vel_axial, vel_radial, swirl_rate, col_width, row_height, stiffness, stiff_elem,
    mass, azim_weight, wall_flag, transfer,
):
    modes = coeff.shape[1]
    planes = vel_axial.shape[1]
    vmem = pl.BlockSpec(memory_space=pltpu.VMEM)
    smem = pl.BlockSpec(memory_space=pltpu.SMEM)
    anywhere = pl.BlockSpec(memory_space=pl.ANY)
    dma = pltpu.SemaphoreType.DMA
    field = pltpu.VMEM((modes, NODES, 128), F32)
    flat = pltpu.VMEM((NODES * modes, 128), F32)
    result = pl.pallas_call(
        functools.partial(kernel, modes),
        out_shape=jax.ShapeDtypeStruct((NODES * modes, 128), F32),
        in_specs=[
            vmem, anywhere, anywhere, anywhere, anywhere, smem, smem, vmem, vmem, vmem, vmem, smem,
            smem,
        ],
        out_specs=vmem,
        scratch_shapes=[
            pltpu.VMEM((3, 4, planes, 128), BF16),
            pltpu.VMEM(tables.shape, BF16),
            flat,
            pltpu.VMEM((RING, 2, 3, 8 * modes, 128), F32),
            pltpu.VMEM((RING * RING, 3, 4 * modes, 128), F32),
            flat,
            flat,
            field,
            field,
            field,
            field,
            field,
            pltpu.VMEM((SWEEPS + 1, 2, 2, SIDE, 128), F32),
            pltpu.VMEM((SWEEPS + 1, 2, 2, SIDE, 128), F32),
            dma((4,)),
            dma((3, 2, 2)),
            dma((3, 2, 2)),
            dma((4, 3)),
            dma((4, 3)),
            dma((15,)),
            dma((15,)),
            dma((SWEEPS + 1, 2)),
            dma((SWEEPS + 1, 2)),
        ],
        compiler_params=pltpu.CompilerParams(collective_id=0, has_side_effects=True),
    )(
        coeff.reshape(NODES * modes, 128),
        swirl_rate,
        vel_radial,
        vel_axial,
        jnp.asarray(tables),
        col_width,
        row_height,
        stiffness,
        stiff_elem.reshape(1, 128),
        mass,
        azim_weight,
        wall_flag,
        transfer,
    )
    return result.reshape(coeff.shape)


def solution(mesh):
    tables = fourier_tables(256)
    return jax.shard_map(
        functools.partial(local, tables),
        mesh=mesh,
        in_specs=(
            P(None, "mode", "elem"),
            P("mode", None, "elem"),
            P("mode", None, "elem"),
            P("mode", None, "elem"),
            P("elem"),
            P(),
            P(),
            P("elem"),
            P(None, "elem"),
            P(None, "elem"),
            P("elem"),
            P("elem"),
        ),
        out_specs=P(None, "mode", "elem"),
        check_vma=False,
    )
```

```python
import functools

import jax
import jax.numpy as jnp
import ml_dtypes
import numpy as np
from jax import lax
from jax.experimental import pallas as pl
from jax.experimental.pallas import tpu as pltpu
from jax.sharding import PartitionSpec as P

MESH = pl.DeviceIdType.MESH
SIDE = 8
NODES = 64
SWEEPS = 3
INV_STEP = 2.0
RELAX = 0.8
RING = 4
F32 = jnp.float32
BF16 = jnp.bfloat16


def cheb_matrix(side_count):
    points = np.cos(np.pi * np.arange(side_count) / (side_count - 1))
    weights = np.ones(side_count)
    weights[0] = weights[-1] = 2.0
    weights = weights * (-1.0) ** np.arange(side_count)
    table = np.zeros((side_count, side_count))
    for row in range(side_count):
        for col in range(side_count):
            if row != col:
                table[row, col] = weights[row] / weights[col] / (points[row] - points[col])
        table[row, row] = -np.sum(table[row])
    return table


def split_table(table):
    high = table.astype(np.float32).astype(ml_dtypes.bfloat16)
    low = (table - high.astype(np.float64)).astype(np.float32).astype(ml_dtypes.bfloat16)
    return [high, low]


def fourier_tables(planes):
    q = np.arange(planes)
    k = (q + 1) // 2
    angle = 2.0 * np.pi / planes * ((k[:, None] * np.arange(planes)[None, :]) % planes)
    sine = ((q % 2 == 0) & (q > 0))[:, None]
    wave = k[:, None].astype(np.float64)
    basis = np.where(sine, np.sin(angle), np.cos(angle))
    slope = np.where(sine, wave * np.cos(angle), -wave * np.sin(angle))
    norm = np.where((q == 0) | (q == planes - 1), 1.0, 2.0) / planes
    forward = basis * norm[:, None]
    return np.stack(split_table(slope.T) + split_table(basis.T) + split_table(forward))


def split(value):
    high = value.astype(BF16)
    return high, (value - high.astype(F32)).astype(BF16)


def dot3(tab_high, tab_low, value):
    high, low = split(value)
    total = jnp.dot(tab_high, high, preferred_element_type=F32)
    total += jnp.dot(tab_high, low, preferred_element_type=F32)
    return total + jnp.dot(tab_low, high, preferred_element_type=F32)


def kernel(
    modes, coeff_in, vel_t, vel_y, vel_x, tables, width_in, height_in, stiff_in, elem_in, mass_in,
    azim_in, flag_in, transfer_in, out,
    coeff, col_width, row_height, stiff, stiff_elem, mass, azim, wall_flag, transfer,
    vel, tab, grad_y, zbuf, xbuf, hat, adv, fld, lam, rate, res, inc, work,
    hsend, hrecv, psend, precv, tsend, halo, far, beside, local_sem, zs, zr, xs, xr, bs, br, hs, hr,
):
    s, m = lax.axis_index("elem"), lax.axis_index("mode")
    elems = lax.axis_size("elem")
    z, x = m // RING, m % RING
    cheb = cheb_matrix(SIDE)

    left, right = lax.rem(s + elems - 1, elems), lax.rem(s + 1, elems)
    barrier = pltpu.get_barrier_semaphore()
    for step in range(1, RING):
        pl.semaphore_signal(
            barrier, inc=1, device_id={"mode": (z + step) % RING * RING + x}, device_id_type=MESH
        )
        pl.semaphore_signal(
            barrier, inc=1, device_id={"mode": z * RING + (x + step) % RING}, device_id_type=MESH
        )
    for other in (left, right):
        pl.semaphore_signal(barrier, inc=1, device_id={"elem": other}, device_id_type=MESH)

    def fetch(pairs):
        copies = [
            pltpu.make_async_copy(src, dst, local_sem.at[i]) for i, (src, dst) in pairs
        ]
        for copy in copies:
            copy.start()
        return copies

    early = fetch(
        enumerate([(coeff_in, coeff), (height_in, row_height), (width_in, col_width)])
    )
    later = fetch(
        enumerate(
            [
                (stiff_in, stiff),
                (elem_in, stiff_elem),
                (mass_in, mass),
                (azim_in, azim),
                (flag_in, wall_flag),
                (transfer_in, transfer),
                (vel_t, vel.at[0]),
                (vel_y, vel.at[1]),
                (vel_x, vel.at[2]),
                (tables, tab),
            ],
            3,
        )
    )
    for copy in early:
        copy.wait()

    lane = lax.broadcasted_iota(jnp.int32, (1, 128), 1)
    col, row = lane // 16, lane % 16
    width = jnp.zeros((1, 128), F32)
    for a in range(8):
        width = jnp.where(col == a, col_width[a], width)
    height = jnp.zeros((1, 128), F32)
    for b in range(16):
        height = jnp.where(row == b, row_height[b], height)
    scale_x = 2.0 / width
    scale_y = 2.0 / height

    @pl.loop(0, SIDE)
    def _(i):
        start = pl.multiple_of(i * 16, 16)
        cells = [coeff[pl.ds(start + j * 128, 16), :] for j in range(SIDE)]
        for j in range(SIDE):
            total = cheb[j, 0] * cells[0]
            for k in range(1, SIDE):
                total += cheb[j, k] * cells[k]
            grad_y[pl.ds(start + j * 128, 16), :] = total * scale_y

    pl.semaphore_wait(barrier, 2 * (RING - 1) + 2)

    own_row = x // 2
    rows = (1 - own_row, own_row)
    zcopy = {}

    def start_z(d, rr):
        target = (z + d) % RING
        block = pl.ds(pl.multiple_of((target * 2 + rows[rr]) * 128, 128), 128)
        for kind, src in ((0, coeff), (1, grad_y)):
            copy = pltpu.make_async_remote_copy(
                src_ref=src.at[block],
                dst_ref=zbuf.at[z, rows[rr], kind],
                send_sem=zs.at[d - 1, rr, kind],
                recv_sem=zr.at[d - 1, rr, kind],
                device_id={"mode": target * RING + x},
                device_id_type=MESH,
            )
            copy.start()
            zcopy[d, rr, kind] = copy

    for rr in range(2):
        start_z(1, rr)
        start_z(3, rr)
    for rr in range(2):
        start_z(2, rr)

    partner = {1: x + 1 - 2 * (x % 2), 2: (x + 2) % RING, 3: RING - 1 - x}
    xcopy = {}

    def pass_on(k, source, rr):
        line = rows[rr]
        cells = [zbuf[source, line, 0, 16 * i : 16 * i + 16, :] for i in range(SIDE)]
        for i in range(SIDE):
            total = cheb[i, 0] * cells[0]
            for j in range(1, SIDE):
                total += cheb[i, j] * cells[j]
            zbuf[source, line, 2, 16 * i : 16 * i + 16, :] = total * scale_x
        for mask in (2, 3) if rr == 0 else (1,):
            target = partner[mask]
            copy = pltpu.make_async_remote_copy(
                src_ref=zbuf.at[source, line, :, pl.ds(pl.multiple_of(target % 2 * 64, 64), 64)],
                dst_ref=xbuf.at[source * RING + x],
                send_sem=xs.at[k, mask - 1],
                recv_sem=xr.at[k, mask - 1],
                device_id={"mode": z * RING + target},
                device_id_type=MESH,
            )
            copy.start()
            xcopy[k, mask] = copy
        if rr == 1:
            xbuf[source * RING + x] = zbuf[
                source, line, :, pl.ds(pl.multiple_of(x % 2 * 64, 64), 64), :
            ]

    for rr in range(2):
        block = pl.ds(pl.multiple_of((z * 2 + rows[rr]) * 128, 128), 128)
        zbuf[z, rows[rr], 0] = coeff[block, :]
        zbuf[z, rows[rr], 1] = grad_y[block, :]
        pass_on(0, z, rr)

    for copy in later[:6]:
        copy.wait()
    flow = jnp.zeros((1, 128), F32)
    for a in range(8):
        flow = jnp.where(col == a, wall_flag[a].astype(F32) * transfer[a], flow)
    flow = jnp.where(row == 0, flow, 0.0)
    elem_scale = stiff_elem[...]
    ones = mass[...]
    weights = azim[...]
    node = lax.broadcasted_iota(jnp.int32, (NODES, 128), 0)
    wall = jnp.where(node < SIDE, jnp.broadcast_to(flow, (NODES, 128)), 0.0)
    stiffness = stiff[...]
    on_diag = lax.broadcasted_iota(jnp.int32, (NODES, NODES), 0) == lax.broadcasted_iota(
        jnp.int32, (NODES, NODES), 1
    )
    stiff_diag = jnp.sum(jnp.where(on_diag, stiffness, 0.0), axis=1, keepdims=True) * elem_scale
    stiff_high, stiff_low = split(stiffness)

    def spread(first, second):
        both = dot3(stiff_high, stiff_low, jnp.concatenate([first, second], axis=1))
        return both[:, :128], both[:, 128:]

    for q in range(modes):
        wave = ((m * modes + q + 1) // 2).astype(F32) * (2.0 / (modes * RING * RING))
        lam[q] = (INV_STEP + (wave * wave) * weights) * ones + wall
        rate[q] = stiff_diag + lam[q]
        fld[q] = coeff[pl.ds(q, NODES, stride=modes), :]

    first_nodes = pl.ds(0, SIDE, stride=SIDE)
    last_nodes = pl.ds(SIDE - 1, SIDE, stride=SIDE)
    has_left = (s > 0).astype(F32)
    has_right = (s < elems - 1).astype(F32)

    def turn(value, shift):
        return pltpu.roll(value, shift % 128, 1) if shift % 128 else value

    def swap(mine, theirs, turn_id):
        copies = []
        for side, other in ((0, left), (1, right)):
            copy = pltpu.make_async_remote_copy(
                src_ref=mine.at[side],
                dst_ref=theirs.at[1 - side],
                send_sem=hs.at[turn_id, side],
                recv_sem=hr.at[turn_id, 1 - side],
                device_id={"elem": other},
                device_id_type=MESH,
            )
            copy.start()
            copies.append(copy)
        return copies

    def join_rows(values, q):
        lower = values[q, 0:SIDE, :]
        upper = values[q, NODES - SIDE : NODES, :]
        values[q, 0:SIDE, :] = lower + jnp.where(row > 0, turn(upper, 1), 0.0)
        values[q, NODES - SIDE : NODES, :] = upper + jnp.where(row < 15, turn(lower, -1), 0.0)

    for g in range(2):
        first = jnp.zeros((SIDE, 128), F32)
        last = jnp.zeros((SIDE, 128), F32)
        for k in range(8):
            first = jnp.where(col == k, turn(rate[8 * g + k, first_nodes, :], 16 * k), first)
            last = jnp.where(col == k, turn(rate[8 * g + k, last_nodes, :], 16 * k + 16), last)
        hsend[0, g] = first
        hsend[1, g] = last
    diag_copies = swap(hsend, hrecv, 0)
    for pair in range(modes // 2):
        applied = spread(fld[2 * pair], fld[2 * pair + 1])
        for h in range(2):
            q = 2 * pair + h
            res[q] = (INV_STEP * ones - lam[q]) * fld[q] - elem_scale * applied[h]
    for copy in diag_copies:
        copy.wait()
    for q in range(modes):
        g, k = q // 8, q % 8
        low, high = rate[q, first_nodes, :], rate[q, last_nodes, :]
        near = turn(hrecv[0, g] * has_left, -16 * k)
        past = turn(hrecv[1, g] * has_right, 112 - 16 * k)
        rate[q, first_nodes, :] = low + jnp.where(col == 0, near, turn(high, 16))
        rate[q, last_nodes, :] = high + jnp.where(col == 7, past, turn(low, -16))
        join_rows(rate, q)
        rate[q] = RELAX / rate[q]

    quad = lane // 32
    outer = col % 2

    def pack(values, send, slot):
        for g in range(modes // 4):
            for side in range(2):
                total = None
                for k in range(4):
                    piece = turn(values[4 * g + k], 32 * k + 32 * side)
                    total = piece if total is None else jnp.where(quad == k, piece, total)
                send[side, slot + g] = total

    pack(lam, psend, 0)
    pack(rate, psend, 4)
    for side in range(2):
        total = None
        for k in range(4):
            piece = turn(elem_scale, 32 * k + 32 * side)
            total = piece if total is None else jnp.where(quad == k, piece, total)
        psend[side, 8] = jnp.broadcast_to(total, (NODES, 128))
    halo_copies = swap(psend, precv, 1)

    def join_inner(values):
        for q in range(modes):
            low, high = values[q, first_nodes, :], values[q, last_nodes, :]
            values[q, first_nodes, :] = low + jnp.where(col == 0, 0.0, turn(high, 16))
            values[q, last_nodes, :] = high + jnp.where(col == 7, 0.0, turn(low, -16))

    def join_halo(values, beside, inner, both):
        for g in range(modes // 4):
            left_low, left_high = beside[0, g, first_nodes, :], beside[0, g, last_nodes, :]
            right_low, right_high = beside[1, g, first_nodes, :], beside[1, g, last_nodes, :]
            add_left = turn(left_low, -16)
            add_right = turn(right_high, 16)
            for k in range(4):
                q = 4 * g + k
                low, high = values[q, first_nodes, :], values[q, last_nodes, :]
                near = turn(left_high * has_left, -32 * k - 16)
                past = turn(right_low * has_right, 112 - 32 * k)
                values[q, first_nodes, :] = jnp.where(col == 0, low + near, low)
                values[q, last_nodes, :] = jnp.where(col == 7, high + past, high)
                if both:
                    add_left = jnp.where(col == 2 * k + 1, turn(low, 32 * k + 16), add_left)
                    add_right = jnp.where(col == 2 * k, turn(high, 32 * k + 16), add_right)
            if both:
                if not inner:
                    add_left = jnp.where(outer == 1, add_left, 0.0)
                    add_right = jnp.where(outer == 0, add_right, 0.0)
                beside[0, g, last_nodes, :] = left_high + add_left
                beside[1, g, first_nodes, :] = right_low + add_right
                if inner:
                    beside[0, g, first_nodes, :] = left_low + jnp.where(
                        outer == 1, turn(left_high, 16), 0.0
                    )
                    beside[1, g, last_nodes, :] = right_high + jnp.where(
                        outer == 0, turn(right_low, -16), 0.0
                    )
        for q in range(modes):
            join_rows(values, q)
        if both:
            for side in range(2):
                for g in range(modes // 4):
                    join_rows(beside.at[side], g)

    for k, d in ((1, 1), (2, 3), (3, 2)):
        for rr in range(2):
            for kind in range(2):
                zcopy[d, rr, kind].wait_recv()
            pass_on(k, (z - d + RING) % RING, rr)

    for copy in later[6:]:
        copy.wait()
    for copy in xcopy.values():
        copy.wait_recv()

    for pair in range(2):
        advect = None
        for kind in range(3):
            pieces = [
                xbuf[:, kind, 32 * pair + 16 * h : 32 * pair + 16 * h + 16, :].reshape(-1, 128)
                for h in range(2)
            ]
            which = 0 if kind == 0 else 2
            phys = dot3(tab[which], tab[which + 1], jnp.concatenate(pieces, axis=1))
            speed = jnp.concatenate([vel[kind, 2 * pair], vel[kind, 2 * pair + 1]], axis=1)
            term = speed.astype(F32) * phys
            advect = term if advect is None else advect + term
        back = dot3(tab[4], tab[5], advect)
        for h in range(2):
            for t in range(RING * RING):
                at = t * 64 + (2 * pair + h) * 16
                hat[at : at + 16, :] = back[16 * t : 16 * t + 16, 128 * h : 128 * h + 128]

    mine = pl.ds(pl.multiple_of(m * 64, 64), 64)
    bcopy = []
    for d in range(1, RING * RING):
        target = (m + d) % (RING * RING)
        copy = pltpu.make_async_remote_copy(
            src_ref=hat.at[pl.ds(pl.multiple_of(target * 64, 64), 64)],
            dst_ref=adv.at[mine],
            send_sem=bs.at[d - 1],
            recv_sem=br.at[d - 1],
            device_id={"mode": target},
            device_id_type=MESH,
        )
        copy.start()
        bcopy.append(copy)
    adv[mine, :] = hat[mine, :]
    for copy in bcopy:
        copy.wait_recv()

    for q in range(modes):
        res[q] = res[q] - ones * adv[pl.ds(q, NODES, stride=modes), :]
    join_inner(res)
    pack(res, tsend, 0)
    for copy in halo_copies:
        copy.wait()
    for copy in swap(tsend, halo, 2):
        copy.wait()
    join_halo(res, halo, False, True)

    for q in range(modes):
        inc[q] = rate[q] * res[q]
    for side in range(2):
        for g in range(modes // 4):
            far[side, g] = precv[side, 4 + g] * halo[side, g]
    for sweep in range(1, SWEEPS):
        for pair in range(modes // 2):
            applied = spread(inc[2 * pair], inc[2 * pair + 1])
            for h in range(2):
                q = 2 * pair + h
                work[q] = elem_scale * applied[h] + lam[q] * inc[q]
        for side in range(2):
            for pair in range(modes // 8):
                applied = spread(far[side, 2 * pair], far[side, 2 * pair + 1])
                for h in range(2):
                    g = 2 * pair + h
                    beside[side, g] = precv[side, 8] * applied[h] + precv[side, g] * far[side, g]
        join_inner(work)
        join_halo(work, beside, True, sweep < SWEEPS - 1)
        for q in range(modes):
            total = inc[q] + rate[q] * (res[q] - work[q])
            if sweep < SWEEPS - 1:
                inc[q] = total
            else:
                out[pl.ds(q, NODES, stride=modes), :] = fld[q] + total
        if sweep < SWEEPS - 1:
            for side in range(2):
                for g in range(modes // 4):
                    far[side, g] = far[side, g] + precv[side, 4 + g] * (
                        halo[side, g] - beside[side, g]
                    )

    for copies in (zcopy, xcopy):
        for copy in copies.values():
            copy.wait_send()
    for copy in bcopy:
        copy.wait_send()


def local(
    tables, coeff, vel_axial, vel_radial, swirl_rate, col_width, row_height, stiffness, stiff_elem,
    mass, azim_weight, wall_flag, transfer,
):
    modes = coeff.shape[1]
    planes = vel_axial.shape[1]
    dma = pltpu.SemaphoreType.DMA
    field = pltpu.VMEM((modes, NODES, 128), F32)
    flat = pltpu.VMEM((NODES * modes, 128), F32)
    columns = pltpu.VMEM((2, modes // 4, NODES, 128), F32)
    outer = pltpu.VMEM((2, modes // 2 + 1, NODES, 128), F32)
    edges = pltpu.VMEM((2, 2, SIDE, 128), F32)
    operands = (
        coeff.reshape(NODES * modes, 128),
        swirl_rate,
        vel_radial,
        vel_axial,
        jnp.asarray(tables),
        col_width,
        row_height,
        stiffness,
        stiff_elem.reshape(1, 128),
        mass,
        azim_weight,
        wall_flag,
        transfer,
    )
    result = pl.pallas_call(
        functools.partial(kernel, modes),
        out_shape=jax.ShapeDtypeStruct((NODES * modes, 128), F32),
        in_specs=[pl.BlockSpec(memory_space=pl.ANY)] * len(operands),
        out_specs=pl.BlockSpec(memory_space=pltpu.VMEM),
        scratch_shapes=[
            flat,
            pltpu.SMEM(col_width.shape, F32),
            pltpu.SMEM(row_height.shape, F32),
            pltpu.VMEM((NODES, NODES), F32),
            pltpu.VMEM((1, 128), F32),
            pltpu.VMEM((NODES, 128), F32),
            pltpu.VMEM((NODES, 128), F32),
            pltpu.SMEM(wall_flag.shape, jnp.int32),
            pltpu.SMEM(transfer.shape, F32),
            pltpu.VMEM((3, 4, planes, 128), BF16),
            pltpu.VMEM(tables.shape, BF16),
            flat,
            pltpu.VMEM((RING, 2, 3, 8 * modes, 128), F32),
            pltpu.VMEM((RING * RING, 3, 4 * modes, 128), F32),
            flat,
            flat,
            field,
            field,
            field,
            field,
            field,
            field,
            edges,
            edges,
            outer,
            outer,
            columns,
            columns,
            columns,
            columns,
            dma((13,)),
            dma((3, 2, 2)),
            dma((3, 2, 2)),
            dma((4, 3)),
            dma((4, 3)),
            dma((15,)),
            dma((15,)),
            dma((3, 2)),
            dma((3, 2)),
        ],
        compiler_params=pltpu.CompilerParams(collective_id=0, has_side_effects=True),
    )(*operands)
    return result.reshape(coeff.shape)


def solution(mesh):
    tables = fourier_tables(256)
    return jax.shard_map(
        functools.partial(local, tables),
        mesh=mesh,
        in_specs=(
            P(None, "mode", "elem"),
            P("mode", None, "elem"),
            P("mode", None, "elem"),
            P("mode", None, "elem"),
            P("elem"),
            P(),
            P(),
            P("elem"),
            P(None, "elem"),
            P(None, "elem"),
            P("elem"),
            P("elem"),
        ),
        out_specs=P(None, "mode", "elem"),
        check_vma=False,
    )
```

```python
import functools

import jax
import jax.numpy as jnp
import ml_dtypes
import numpy as np
from jax import lax
from jax.experimental import pallas as pl
from jax.experimental.pallas import tpu as pltpu
from jax.sharding import PartitionSpec as P

MESH = pl.DeviceIdType.MESH
SIDE = 8
NODES = 64
SWEEPS = 3
INV_STEP = 2.0
RELAX = 0.8
RING = 4
F32 = jnp.float32
BF16 = jnp.bfloat16


def cheb_matrix(side_count):
    points = np.cos(np.pi * np.arange(side_count) / (side_count - 1))
    weights = np.ones(side_count)
    weights[0] = weights[-1] = 2.0
    weights = weights * (-1.0) ** np.arange(side_count)
    table = np.zeros((side_count, side_count))
    for row in range(side_count):
        for col in range(side_count):
            if row != col:
                table[row, col] = weights[row] / weights[col] / (points[row] - points[col])
        table[row, row] = -np.sum(table[row])
    return table


def split_table(table):
    high = table.astype(np.float32).astype(ml_dtypes.bfloat16)
    low = (table - high.astype(np.float64)).astype(np.float32).astype(ml_dtypes.bfloat16)
    return [high, low]


def fourier_tables(planes):
    q = np.arange(planes)
    k = (q + 1) // 2
    angle = 2.0 * np.pi / planes * ((k[:, None] * np.arange(planes)[None, :]) % planes)
    sine = ((q % 2 == 0) & (q > 0))[:, None]
    wave = k[:, None].astype(np.float64)
    basis = np.where(sine, np.sin(angle), np.cos(angle))
    slope = np.where(sine, wave * np.cos(angle), -wave * np.sin(angle))
    norm = np.where((q == 0) | (q == planes - 1), 1.0, 2.0) / planes
    forward = basis * norm[:, None]
    return np.stack(split_table(slope.T) + split_table(basis.T) + split_table(forward))


def split(value):
    high = value.astype(BF16)
    return high, (value - high.astype(F32)).astype(BF16)


def dot3(tab_high, tab_low, value):
    high, low = split(value)
    total = jnp.dot(tab_high, high, preferred_element_type=F32)
    total += jnp.dot(tab_high, low, preferred_element_type=F32)
    return total + jnp.dot(tab_low, high, preferred_element_type=F32)


def kernel(
    modes, coeff_in, vel_t, vel_y, vel_x, tables, width_in, height_in, stiff_in, elem_in, mass_in,
    azim_in, flag_in, transfer_in, out,
    coeff, col_width, row_height, stiff, stiff_elem, traits, wall_flag, transfer,
    vel, tab, grad_y, zc, zg, zx, xc, xx, xy, hat, adv, fld, lam, rate, res, inc, work,
    theirs, side_lam, side_rate, tsend, halo, far, beside, local_sem, zs, zr, xs, xr, bs, br, hs, hr,
):
    s, m = lax.axis_index("elem"), lax.axis_index("mode")
    elems = lax.axis_size("elem")
    z, x = m // RING, m % RING
    cheb = cheb_matrix(SIDE)

    left, right = lax.max(s - 1, 0), lax.min(s + 1, elems - 1)
    has_left, has_right = s > 0, s < elems - 1
    barrier = pltpu.get_barrier_semaphore()
    for step in range(1, RING):
        pl.semaphore_signal(
            barrier, inc=1, device_id={"mode": (z + step) % RING * RING + x}, device_id_type=MESH
        )
        pl.semaphore_signal(
            barrier, inc=1, device_id={"mode": z * RING + (x + step) % RING}, device_id_type=MESH
        )
    for other, there in ((left, has_left), (right, has_right)):

        @pl.when(there)
        def _():
            pl.semaphore_signal(barrier, inc=1, device_id={"elem": other}, device_id_type=MESH)


    def fetch(pairs):
        copies = [
            pltpu.make_async_copy(src, dst, local_sem.at[i]) for i, (src, dst) in pairs
        ]
        for copy in copies:
            copy.start()
        return copies

    early = fetch(
        enumerate([(coeff_in, coeff), (height_in, row_height), (width_in, col_width)])
    )
    later = fetch(
        enumerate(
            [
                (stiff_in, stiff),
                (elem_in, stiff_elem),
                (mass_in, traits.at[pl.ds(0, NODES)]),
                (azim_in, traits.at[pl.ds(NODES, NODES)]),
                (flag_in, wall_flag),
                (transfer_in, transfer),
                (vel_t, vel.at[0]),
                (vel_y, vel.at[1]),
                (vel_x, vel.at[2]),
                (tables, tab),
            ],
            3,
        )
    )
    for copy in early:
        copy.wait()

    lane = lax.broadcasted_iota(jnp.int32, (1, 128), 1)
    col, row = lane // 16, lane % 16
    width = jnp.zeros((1, 128), F32)
    for a in range(8):
        width = jnp.where(col == a, col_width[a], width)
    height = jnp.zeros((1, 128), F32)
    for b in range(16):
        height = jnp.where(row == b, row_height[b], height)
    scale_x = 2.0 / width
    scale_y = 2.0 / height

    @pl.loop(0, SIDE)
    def _(i):
        start = pl.multiple_of(i * 16, 16)
        cells = [coeff[pl.ds(start + j * 128, 16), :] for j in range(SIDE)]
        place = pl.multiple_of(i % 4 // 2 * 64 + i // 4 * 32 + i % 2 * 16, 16)
        for j in range(SIDE):
            total = cheb[j, 0] * cells[0]
            for k in range(1, SIDE):
                total += cheb[j, k] * cells[k]
            grad_y[pl.ds(place + j * 128, 16), :] = total * scale_y

    pl.semaphore_wait(
        barrier, 2 * (RING - 1) + has_left.astype(jnp.int32) + has_right.astype(jnp.int32)
    )

    own_row = x // 2
    rows = (1 - own_row, own_row)
    zcopy, xcopy = {}, {}
    waves = [(rr, d) for rr in range(2) for d in (1, 3)] + [(rr, 2) for rr in range(2)]
    lots = ((1, 1), (2, 3), (3, 2))

    def row_start(plane, rr):
        return (plane * 2 + rows[rr]) * 128

    def start_z(what, d, rr, src, dst):
        copy = pltpu.make_async_remote_copy(
            src_ref=src,
            dst_ref=dst,
            send_sem=zs.at[what, d - 1, rr],
            recv_sem=zr.at[what, d - 1, rr],
            device_id={"mode": (z + d) % RING * RING + x},
            device_id_type=MESH,
        )
        copy.start()
        zcopy[what, d, rr] = copy

    def swap(pairs, turn_id):
        copies = []
        for side, other, there in ((0, left, has_left), (1, right, has_right)):
            copy = pltpu.make_async_remote_copy(
                src_ref=pairs[side][0],
                dst_ref=pairs[side][1],
                send_sem=hs.at[turn_id, side],
                recv_sem=hr.at[turn_id, 1 - side],
                device_id={"elem": other},
                device_id_type=MESH,
            )
            pl.when(there)(copy.start)
            copies.append(copy)
        return copies

    def settle(copies, theirs):
        for side, there in ((0, has_left), (1, has_right)):

            @pl.when(there)
            def _():
                copies[side].wait_send()
                copies[1 - side].wait_recv()

            @pl.when(jnp.logical_not(there))
            def _():
                theirs[side] = jnp.zeros(theirs.shape[1:], F32)

    for copy in later[:6]:
        copy.wait()
    flow = jnp.zeros((1, 128), F32)
    for a in range(8):
        flow = jnp.where(col == a, wall_flag[a].astype(F32) * transfer[a], flow)
    flow = jnp.where(row == 0, flow, 0.0)
    elem_scale = stiff_elem[...]
    line8 = lax.broadcasted_iota(jnp.int32, (SIDE, 128), 0)
    traits[2 * NODES : 2 * NODES + SIDE, :] = jnp.where(line8 == 0, elem_scale, flow)
    trait_copies = swap([(traits, theirs.at[1]), (traits, theirs.at[0])], 0)

    for rr, d in waves:
        at = pl.ds(pl.multiple_of(row_start((z + d) % RING, rr), 128), 128)
        start_z(0, d, rr, coeff.at[at], zc.at[z, rows[rr]])
    for part in range(2):
        for rr, d in waves:
            at = pl.ds(pl.multiple_of(row_start((z + d) % RING, rr) + 64 * part, 64), 64)
            start_z(1 + part, d, rr, grad_y.at[at], zg.at[z, rows[rr], part])

    partner = {1: x + 1 - 2 * (x % 2), 2: (x + 2) % RING, 3: RING - 1 - x}

    def start_x(what, k, mask, src, dst):
        copy = pltpu.make_async_remote_copy(
            src_ref=src,
            dst_ref=dst,
            send_sem=xs.at[what, k, mask - 1],
            recv_sem=xr.at[what, k, mask - 1],
            device_id={"mode": z * RING + partner[mask]},
            device_id_type=MESH,
        )
        copy.start()
        xcopy[what, k, mask] = copy

    def half(target, size):
        return pl.ds(pl.multiple_of(target % 2 * size, size), size)

    def pass_values(k, source, rr, line):
        cells = [line[16 * i : 16 * i + 16, :] for i in range(SIDE)]
        slopes = zx.at[source, rows[rr]]
        for i in range(SIDE):
            total = cheb[i, 0] * cells[0]
            for j in range(1, SIDE):
                total += cheb[i, j] * cells[j]
            slopes[16 * i : 16 * i + 16, :] = total * scale_x
        spot = source * RING + x
        for what, src, dst in ((0, line, xc), (1, slopes, xx)):
            for mask in (2, 3) if rr == 0 else (1,):
                start_x(what, k, mask, src.at[half(partner[mask], 64)], dst.at[spot])
            if rr == 1:
                dst[spot] = src[half(x, 64), :]

    def pass_grad(k, source, rr, part, line):
        spot = source * RING + x
        for mask in (2, 3) if rr == 0 else (1,):
            start_x(2 + part, k, mask, line.at[half(partner[mask], 32)], xy.at[spot, part])
        if rr == 1:
            xy[spot, part] = line[half(x, 32), :]

    for rr in range(2):
        at = pl.multiple_of(row_start(z, rr), 128)
        pass_values(0, z, rr, coeff.at[pl.ds(at, 128)])
        for part in range(2):
            pass_grad(0, z, rr, part, grad_y.at[pl.ds(at + 64 * part, 64)])

    ones = traits[0:NODES, :]
    weights = traits[NODES : 2 * NODES, :]
    node = lax.broadcasted_iota(jnp.int32, (NODES, 128), 0)
    stiffness = stiff[...]
    on_diag = lax.broadcasted_iota(jnp.int32, (NODES, NODES), 0) == lax.broadcasted_iota(
        jnp.int32, (NODES, NODES), 1
    )
    stiff_diag = jnp.sum(jnp.where(on_diag, stiffness, 0.0), axis=1, keepdims=True)
    stiff_high, stiff_low = split(stiffness)

    def spread(first, second):
        both = dot3(stiff_high, stiff_low, jnp.concatenate([first, second], axis=1))
        return both[:, :128], both[:, 128:]

    def local_terms(lumped, inverse, rates, scale, lam_to, diag_to):
        wall = jnp.where(node < SIDE, jnp.broadcast_to(rates, (NODES, 128)), 0.0)
        stiff_part = stiff_diag * scale
        for q in range(modes):
            wave = ((m * modes + q + 1) // 2).astype(F32) * (2.0 / (modes * RING * RING))
            value = (INV_STEP + (wave * wave) * inverse) * lumped + wall
            lam_to[q] = value
            diag_to[q] = stiff_part + value

    local_terms(ones, weights, flow, elem_scale, lam, rate)
    for q in range(modes):
        fld[q] = coeff[pl.ds(q, NODES, stride=modes), :]

    first_nodes = pl.ds(0, SIDE, stride=SIDE)
    last_nodes = pl.ds(SIDE - 1, SIDE, stride=SIDE)
    def turn(value, shift):
        return pltpu.roll(value, shift % 128, 1) if shift % 128 else value

    def join_rows(values, q):
        lower = values[q, 0:SIDE, :]
        upper = values[q, NODES - SIDE : NODES, :]
        values[q, 0:SIDE, :] = lower + jnp.where(row > 0, turn(upper, 1), 0.0)
        values[q, NODES - SIDE : NODES, :] = upper + jnp.where(row < 15, turn(lower, -1), 0.0)

    for pair in range(modes // 2):
        applied = spread(fld[2 * pair], fld[2 * pair + 1])
        for h in range(2):
            q = 2 * pair + h
            res[q] = (INV_STEP * ones - lam[q]) * fld[q] - elem_scale * applied[h]
    quad = lane // 32
    outer = col % 2

    def pack(pieces, send, shift):
        for g in range(len(pieces) // 4):
            total = None
            for k in range(4):
                piece = turn(pieces[4 * g + k], 32 * k + shift)
                total = piece if total is None else jnp.where(quad == k, piece, total)
            send[g] = total

    def join_inner(values):
        for q in range(modes):
            low, high = values[q, first_nodes, :], values[q, last_nodes, :]
            values[q, first_nodes, :] = low + jnp.where(col == 0, 0.0, turn(high, 16))
            values[q, last_nodes, :] = high + jnp.where(col == 7, 0.0, turn(low, -16))

    def join_halo(values, beside, inner, both):
        for g in range(modes // 4):
            left_low, left_high = beside[0, g, first_nodes, :], beside[0, g, last_nodes, :]
            right_low, right_high = beside[1, g, first_nodes, :], beside[1, g, last_nodes, :]
            add_left = turn(left_low, -16)
            add_right = turn(right_high, 16)
            for k in range(4):
                q = 4 * g + k
                low, high = values[q, first_nodes, :], values[q, last_nodes, :]
                near = turn(left_high, -32 * k - 16)
                past = turn(right_low, 112 - 32 * k)
                values[q, first_nodes, :] = jnp.where(col == 0, low + near, low)
                values[q, last_nodes, :] = jnp.where(col == 7, high + past, high)
                if both:
                    add_left = jnp.where(col == 2 * k + 1, turn(low, 32 * k + 16), add_left)
                    add_right = jnp.where(col == 2 * k, turn(high, 32 * k + 16), add_right)
            if both:
                if not inner:
                    add_left = jnp.where(outer == 1, add_left, 0.0)
                    add_right = jnp.where(outer == 0, add_right, 0.0)
                beside[0, g, last_nodes, :] = left_high + add_left
                beside[1, g, first_nodes, :] = right_low + add_right
                if inner:
                    beside[0, g, first_nodes, :] = left_low + jnp.where(
                        outer == 1, turn(left_high, 16), 0.0
                    )
                    beside[1, g, last_nodes, :] = right_high + jnp.where(
                        outer == 0, turn(right_low, -16), 0.0
                    )
        for q in range(modes):
            join_rows(values, q)
        if both:
            for side in range(2):
                for g in range(modes // 4):
                    join_rows(beside.at[side], g)

    for k, d in lots:
        source = (z - d + RING) % RING
        for rr in range(2):
            zcopy[0, d, rr].wait_recv()
            pass_values(k, source, rr, zc.at[source, rows[rr]])

    settle(trait_copies, theirs)
    join_inner(rate)
    side_scale = []
    here = lane >= 64
    for side in range(2):
        def window(mine, others):
            return jnp.where(here == (side == 0), turn(mine, 64), turn(others, 64))

        local_terms(
            window(ones, theirs[side, 0:NODES, :]),
            window(weights, theirs[side, NODES : 2 * NODES, :]),
            window(flow, theirs[side, 2 * NODES + 1 : 2 * NODES + 2, :]),
            window(elem_scale, theirs[side, 2 * NODES : 2 * NODES + 1, :]),
            work,
            inc,
        )
        join_inner(inc)
        for q in range(modes):
            at = first_nodes if side == 0 else last_nodes
            value = turn(inc[q, at, :], 64)
            rate[q, at, :] = jnp.where(col == (0 if side == 0 else 7), value, rate[q, at, :])
            join_rows(inc, q)
            inc[q] = RELAX / inc[q]
        shift = -32 if side == 0 else -64
        pack([work[q] for q in range(modes)], side_lam.at[side], shift)
        pack([inc[q] for q in range(modes)], side_rate.at[side], shift)

        @pl.when(jnp.logical_not(has_left if side == 0 else has_right))
        def _():
            side_rate[side] = jnp.zeros(side_rate.shape[1:], F32)

        scales = window(elem_scale, theirs[side, 2 * NODES : 2 * NODES + 1, :])
        total = None
        for k in range(4):
            piece = turn(scales, 32 * k + shift)
            total = piece if total is None else jnp.where(quad == k, piece, total)
        side_scale.append(total)
    for q in range(modes):
        join_rows(rate, q)
        rate[q] = RELAX / rate[q]

    bcopy = []
    for part in range(2):
        for k, d in lots:
            source = (z - d + RING) % RING
            for rr in range(2):
                zcopy[1 + part, d, rr].wait_recv()
                pass_grad(k, source, rr, part, zg.at[source, rows[rr], part])
        if part == 0:
            for copy in later[6:]:
                copy.wait()
        for (what, k, mask), copy in xcopy.items():
            if what == 2 + part or (what < 2 and part == 0):
                copy.wait_recv()
        advect = None
        for kind, src in enumerate((xc, xy, xx)):
            pieces = []
            for h in range(2):
                at = 32 * part + 16 * h
                piece = src[:, part, 16 * h : 16 * h + 16, :] if kind == 1 else src[:, at : at + 16, :]
                pieces.append(piece.reshape(-1, 128))
            which = 0 if kind == 0 else 2
            phys = dot3(tab[which], tab[which + 1], jnp.concatenate(pieces, axis=1))
            speed = jnp.concatenate([vel[kind, 2 * part], vel[kind, 2 * part + 1]], axis=1)
            term = speed.astype(F32) * phys
            advect = term if advect is None else advect + term
        back = dot3(tab[4], tab[5], advect)
        for h in range(2):
            for t in range(RING * RING):
                hat[part, t, 16 * h : 16 * h + 16, :] = back[
                    16 * t : 16 * t + 16, 128 * h : 128 * h + 128
                ]
        mine = pl.ds(pl.multiple_of(m * 64 + 32 * part, 32), 32)
        for d in range(1, RING * RING):
            target = (m + d) % (RING * RING)
            copy = pltpu.make_async_remote_copy(
                src_ref=hat.at[part, target],
                dst_ref=adv.at[mine],
                send_sem=bs.at[part, d - 1],
                recv_sem=br.at[part, d - 1],
                device_id={"mode": target},
                device_id_type=MESH,
            )
            copy.start()
            bcopy.append(copy)
        adv[mine, :] = hat[part, m]
    for copy in bcopy:
        copy.wait_recv()

    for q in range(modes):
        res[q] = res[q] - ones * adv[pl.ds(q, NODES, stride=modes), :]
    join_inner(res)
    for side in range(2):
        pack([res[q] for q in range(modes)], tsend.at[side], 32 * side)
    settle(swap([(tsend.at[0], halo.at[1]), (tsend.at[1], halo.at[0])], 1), halo)
    join_halo(res, halo, False, True)

    for q in range(modes):
        inc[q] = rate[q] * res[q]
    for side in range(2):
        for g in range(modes // 4):
            far[side, g] = side_rate[side, g] * halo[side, g]
    for sweep in range(1, SWEEPS):
        for pair in range(modes // 2):
            applied = spread(inc[2 * pair], inc[2 * pair + 1])
            for h in range(2):
                q = 2 * pair + h
                work[q] = elem_scale * applied[h] + lam[q] * inc[q]
        for side in range(2):
            for pair in range(modes // 8):
                applied = spread(far[side, 2 * pair], far[side, 2 * pair + 1])
                for h in range(2):
                    g = 2 * pair + h
                    beside[side, g] = side_scale[side] * applied[h] + side_lam[side, g] * far[side, g]
        join_inner(work)
        join_halo(work, beside, True, sweep < SWEEPS - 1)
        for q in range(modes):
            total = inc[q] + rate[q] * (res[q] - work[q])
            if sweep < SWEEPS - 1:
                inc[q] = total
            else:
                out[pl.ds(q, NODES, stride=modes), :] = fld[q] + total
        if sweep < SWEEPS - 1:
            for side in range(2):
                for g in range(modes // 4):
                    far[side, g] = far[side, g] + side_rate[side, g] * (
                        halo[side, g] - beside[side, g]
                    )

    for copies in (zcopy, xcopy):
        for copy in copies.values():
            copy.wait_send()
    for copy in bcopy:
        copy.wait_send()


def local(
    tables, coeff, vel_axial, vel_radial, swirl_rate, col_width, row_height, stiffness, stiff_elem,
    mass, azim_weight, wall_flag, transfer,
):
    modes = coeff.shape[1]
    planes = vel_axial.shape[1]
    dma = pltpu.SemaphoreType.DMA
    field = pltpu.VMEM((modes, NODES, 128), F32)
    flat = pltpu.VMEM((NODES * modes, 128), F32)
    columns = pltpu.VMEM((2, modes // 4, NODES, 128), F32)
    rows = pltpu.VMEM((RING, 2, 8 * modes, 128), F32)
    blocks = pltpu.VMEM((RING * RING, 4 * modes, 128), F32)
    halves = pltpu.VMEM((RING * RING, 2, 2 * modes, 128), F32)
    operands = (
        coeff.reshape(NODES * modes, 128),
        swirl_rate,
        vel_radial,
        vel_axial,
        jnp.asarray(tables),
        col_width,
        row_height,
        stiffness,
        stiff_elem.reshape(1, 128),
        mass,
        azim_weight,
        wall_flag,
        transfer,
    )
    result = pl.pallas_call(
        functools.partial(kernel, modes),
        out_shape=jax.ShapeDtypeStruct((NODES * modes, 128), F32),
        in_specs=[pl.BlockSpec(memory_space=pl.ANY)] * len(operands),
        out_specs=pl.BlockSpec(memory_space=pltpu.VMEM),
        scratch_shapes=[
            flat,
            pltpu.SMEM(col_width.shape, F32),
            pltpu.SMEM(row_height.shape, F32),
            pltpu.VMEM((NODES, NODES), F32),
            pltpu.VMEM((1, 128), F32),
            pltpu.VMEM((2 * NODES + SIDE, 128), F32),
            pltpu.SMEM(wall_flag.shape, jnp.int32),
            pltpu.SMEM(transfer.shape, F32),
            pltpu.VMEM((3, 4, planes, 128), BF16),
            pltpu.VMEM(tables.shape, BF16),
            flat,
            rows,
            pltpu.VMEM((RING, 2, 2, 4 * modes, 128), F32),
            rows,
            blocks,
            blocks,
            halves,
            pltpu.VMEM((2, RING * RING, 2 * modes, 128), F32),
            flat,
            field,
            field,
            field,
            field,
            field,
            field,
            pltpu.VMEM((2, 2 * NODES + SIDE, 128), F32),
            columns,
            columns,
            columns,
            columns,
            columns,
            columns,
            dma((13,)),
            dma((3, 3, 2)),
            dma((3, 3, 2)),
            dma((4, 4, 3)),
            dma((4, 4, 3)),
            dma((2, 15)),
            dma((2, 15)),
            dma((2, 2)),
            dma((2, 2)),
        ],
        compiler_params=pltpu.CompilerParams(collective_id=0, has_side_effects=True),
    )(*operands)
    return result.reshape(coeff.shape)


def solution(mesh):
    tables = fourier_tables(256)
    return jax.shard_map(
        functools.partial(local, tables),
        mesh=mesh,
        in_specs=(
            P(None, "mode", "elem"),
            P("mode", None, "elem"),
            P("mode", None, "elem"),
            P("mode", None, "elem"),
            P("elem"),
            P(),
            P(),
            P("elem"),
            P(None, "elem"),
            P(None, "elem"),
            P("elem"),
            P("elem"),
        ),
        out_specs=P(None, "mode", "elem"),
        check_vma=False,
    )
```

```python
import functools

import jax
import jax.numpy as jnp
import ml_dtypes
import numpy as np
from jax import lax
from jax.experimental import pallas as pl
from jax.experimental.pallas import tpu as pltpu
from jax.sharding import PartitionSpec as P

MESH = pl.DeviceIdType.MESH
SIDE = 8
NODES = 64
SWEEPS = 3
INV_STEP = 2.0
RELAX = 0.8
RING = 4
F32 = jnp.float32
BF16 = jnp.bfloat16


def cheb_matrix(side_count):
    points = np.cos(np.pi * np.arange(side_count) / (side_count - 1))
    weights = np.ones(side_count)
    weights[0] = weights[-1] = 2.0
    weights = weights * (-1.0) ** np.arange(side_count)
    table = np.zeros((side_count, side_count))
    for row in range(side_count):
        for col in range(side_count):
            if row != col:
                table[row, col] = weights[row] / weights[col] / (points[row] - points[col])
        table[row, row] = -np.sum(table[row])
    return table


def split_table(table):
    high = table.astype(np.float32).astype(ml_dtypes.bfloat16)
    low = (table - high.astype(np.float64)).astype(np.float32).astype(ml_dtypes.bfloat16)
    return [high, low]


def fourier_tables(planes):
    q = np.arange(planes)
    k = (q + 1) // 2
    angle = 2.0 * np.pi / planes * ((k[:, None] * np.arange(planes)[None, :]) % planes)
    sine = ((q % 2 == 0) & (q > 0))[:, None]
    wave = k[:, None].astype(np.float64)
    basis = np.where(sine, np.sin(angle), np.cos(angle))
    slope = np.where(sine, wave * np.cos(angle), -wave * np.sin(angle))
    norm = np.where((q == 0) | (q == planes - 1), 1.0, 2.0) / planes
    forward = basis * norm[:, None]
    return np.stack(split_table(slope.T) + split_table(basis.T) + split_table(forward))


def split(value):
    high = value.astype(BF16)
    return high, (value - high.astype(F32)).astype(BF16)


def dot3(tab_high, tab_low, value):
    high, low = split(value)
    total = jnp.dot(tab_high, high, preferred_element_type=F32)
    total += jnp.dot(tab_high, low, preferred_element_type=F32)
    return total + jnp.dot(tab_low, high, preferred_element_type=F32)


def kernel(
    modes, coeff_in, vel_t, vel_y, vel_x, tables, width_in, height_in, stiff_in, elem_in, mass_in,
    azim_in, flag_in, transfer_in, out,
    coeff, col_width, row_height, stiff, stiff_elem, traits, wall_flag, transfer,
    vel, tab, grad_y, ends, far_ends, zc, zg, zx, xc, xx, xy, hat, adv, fld, lam, rate, res, inc, work,
    theirs, side_lam, side_rate, tsend, halo, far, beside, local_sem, zs, zr, xs, xr, bs, br, hs, hr,
):
    s, m = lax.axis_index("elem"), lax.axis_index("mode")
    elems = lax.axis_size("elem")
    z, x = m // RING, m % RING
    cheb = cheb_matrix(SIDE)

    left, right = lax.max(s - 1, 0), lax.min(s + 1, elems - 1)
    has_left, has_right = s > 0, s < elems - 1
    barrier = pltpu.get_barrier_semaphore()
    for step in range(1, RING):
        if step != 2:
            pl.semaphore_signal(
                barrier,
                inc=1,
                device_id={"mode": (z + step) % RING * RING + x},
                device_id_type=MESH,
            )
        pl.semaphore_signal(
            barrier, inc=1, device_id={"mode": z * RING + (x + step) % RING}, device_id_type=MESH
        )
    for other, there in ((left, has_left), (right, has_right)):

        @pl.when(there)
        def _():
            pl.semaphore_signal(barrier, inc=1, device_id={"elem": other}, device_id_type=MESH)


    def fetch(pairs):
        copies = [
            pltpu.make_async_copy(src, dst, local_sem.at[i]) for i, (src, dst) in pairs
        ]
        for copy in copies:
            copy.start()
        return copies

    early = fetch(
        enumerate([(coeff_in, coeff), (height_in, row_height), (width_in, col_width)])
    )
    later = fetch(
        enumerate(
            [
                (stiff_in, stiff),
                (elem_in, stiff_elem),
                (mass_in, traits.at[pl.ds(0, NODES)]),
                (azim_in, traits.at[pl.ds(NODES, NODES)]),
                (flag_in, wall_flag),
                (transfer_in, transfer),
                (vel_t, vel.at[0]),
                (vel_y, vel.at[1]),
                (vel_x, vel.at[2]),
                (tables, tab),
            ],
            3,
        )
    )
    for copy in early:
        copy.wait()

    lane = lax.broadcasted_iota(jnp.int32, (1, 128), 1)
    col, row = lane // 16, lane % 16
    width = jnp.zeros((1, 128), F32)
    for a in range(8):
        width = jnp.where(col == a, col_width[a], width)
    height = jnp.zeros((1, 128), F32)
    for b in range(16):
        height = jnp.where(row == b, row_height[b], height)
    scale_x = 2.0 / width
    scale_y = 2.0 / height

    @pl.loop(0, SIDE)
    def _(i):
        start = pl.multiple_of(i * 16, 16)
        cells = [coeff[pl.ds(start + j * 128, 16), :] for j in range(SIDE)]
        place = pl.multiple_of(i % 4 // 2 * 64 + i // 4 * 32 + i % 2 * 16, 16)
        for j in range(SIDE):
            total = cheb[j, 0] * cells[0]
            for k in range(1, SIDE):
                total += cheb[j, k] * cells[k]
            grad_y[pl.ds(place + j * 128, 16), :] = total * scale_y

    own_row = x // 2
    rows = (1 - own_row, own_row)
    for plane in range(RING):
        tile = jnp.zeros((16, 128), F32)
        for kind, src in ((0, coeff), (1, grad_y)):
            for rr in range(2):
                at = pl.multiple_of((2 * plane + rows[rr]) * 128 + 112, 16)
                edge = pltpu.roll(src[pl.ds(at, 16), :], 32 * kind + 16 * rr + 16, 1)
                tile = jnp.where(col == 2 * kind + rr, edge, tile)
        ends[16 * plane : 16 * plane + 16, :] = tile

    def last_node(first, tile, which):
        return jnp.where(
            lane < 112, pltpu.roll(first, 112, 1), pltpu.roll(tile, 112 - 16 * which, 1)
        )

    pl.semaphore_wait(
        barrier, 2 * RING - 3 + has_left.astype(jnp.int32) + has_right.astype(jnp.int32)
    )

    zcopy, xcopy = {}, {}
    near = [(rr, d) for rr in range(2) for d in (1, 3)]
    waves = near + [(rr, 2) for rr in range(2)]
    lots = ((1, 1), (2, 3), (3, 2))

    def row_start(plane, rr):
        return (plane * 2 + rows[rr]) * 128

    def start_z(what, d, rr, src, dst):
        copy = pltpu.make_async_remote_copy(
            src_ref=src,
            dst_ref=dst,
            send_sem=zs.at[what, d - 1, rr],
            recv_sem=zr.at[what, d - 1, rr],
            device_id={"mode": (z + d) % RING * RING + x},
            device_id_type=MESH,
        )
        copy.start()
        zcopy[what, d, rr] = copy

    def swap(pairs, turn_id):
        copies = []
        for side, other, there in ((0, left, has_left), (1, right, has_right)):
            copy = pltpu.make_async_remote_copy(
                src_ref=pairs[side][0],
                dst_ref=pairs[side][1],
                send_sem=hs.at[turn_id, side],
                recv_sem=hr.at[turn_id, 1 - side],
                device_id={"elem": other},
                device_id_type=MESH,
            )
            pl.when(there)(copy.start)
            copies.append(copy)
        return copies

    def settle(copies, theirs):
        for side, there in ((0, has_left), (1, has_right)):

            @pl.when(there)
            def _():
                copies[side].wait_send()
                copies[1 - side].wait_recv()

            @pl.when(jnp.logical_not(there))
            def _():
                theirs[side] = jnp.zeros(theirs.shape[1:], F32)

    for copy in later[:6]:
        copy.wait()
    flow = jnp.zeros((1, 128), F32)
    for a in range(8):
        flow = jnp.where(col == a, wall_flag[a].astype(F32) * transfer[a], flow)
    flow = jnp.where(row == 0, flow, 0.0)
    elem_scale = stiff_elem[...]
    line8 = lax.broadcasted_iota(jnp.int32, (SIDE, 128), 0)
    traits[2 * NODES : 2 * NODES + SIDE, :] = jnp.where(line8 == 0, elem_scale, flow)
    trait_copies = swap([(traits, theirs.at[1]), (traits, theirs.at[0])], 0)

    def send_values(d, rr):
        if rr == 0:
            at = pl.ds(pl.multiple_of((z + d) % RING * 16, 16), 16)
            start_z(3, d, 0, ends.at[at], far_ends.at[z])
        at = pl.ds(pl.multiple_of(row_start((z + d) % RING, rr), 128), 112)
        start_z(0, d, rr, coeff.at[at], zc.at[z, rows[rr], pl.ds(0, 112)])

    for rr, d in near:
        send_values(d, rr)

    partner = {1: x + 1 - 2 * (x % 2), 2: (x + 2) % RING, 3: RING - 1 - x}

    def start_x(what, k, mask, src, dst):
        copy = pltpu.make_async_remote_copy(
            src_ref=src,
            dst_ref=dst,
            send_sem=xs.at[what, k, mask - 1],
            recv_sem=xr.at[what, k, mask - 1],
            device_id={"mode": z * RING + partner[mask]},
            device_id_type=MESH,
        )
        copy.start()
        xcopy[what, k, mask] = copy

    def half(target, size):
        return pl.ds(pl.multiple_of(target % 2 * size, size), size)

    def pass_values(k, source, rr, line):
        cells = [line[16 * i : 16 * i + 16, :] for i in range(SIDE)]
        slopes = zx.at[source, rows[rr]]
        for i in range(SIDE):
            total = cheb[i, 0] * cells[0]
            for j in range(1, SIDE):
                total += cheb[i, j] * cells[j]
            slopes[16 * i : 16 * i + 16, :] = total * scale_x
        spot = source * RING + x
        for what, src, dst in ((0, line, xc), (1, slopes, xx)):
            for mask in (2, 3) if rr == 0 else (1,):
                start_x(what, k, mask, src.at[half(partner[mask], 64)], dst.at[spot])
            if rr == 1:
                dst[spot] = src[half(x, 64), :]

    def pass_grad(k, source, rr, part, line):
        spot = source * RING + x
        for mask in (2, 3) if rr == 0 else (1,):
            start_x(2 + part, k, mask, line.at[half(partner[mask], 32)], xy.at[spot, part])
        if rr == 1:
            xy[spot, part] = line[half(x, 32), :]

    for rr in range(2):
        at = pl.multiple_of(row_start(z, rr), 128)
        pass_values(0, z, rr, coeff.at[pl.ds(at, 128)])
        for part in range(2):
            pass_grad(0, z, rr, part, grad_y.at[pl.ds(at + 64 * part, 64)])

    zcopy[0, 1, 0].wait_recv()
    for rr in range(2):
        send_values(2, rr)
    for part, size in ((0, 64), (1, 48)):
        for rr, d in waves:
            at = pl.ds(pl.multiple_of(row_start((z + d) % RING, rr) + 64 * part, 64), size)
            start_z(1 + part, d, rr, grad_y.at[at], zg.at[z, rows[rr], part, pl.ds(0, size)])

    ones = traits[0:NODES, :]
    weights = traits[NODES : 2 * NODES, :]
    node = lax.broadcasted_iota(jnp.int32, (NODES, 128), 0)
    stiffness = stiff[...]
    on_diag = lax.broadcasted_iota(jnp.int32, (NODES, NODES), 0) == lax.broadcasted_iota(
        jnp.int32, (NODES, NODES), 1
    )
    stiff_diag = jnp.sum(jnp.where(on_diag, stiffness, 0.0), axis=1, keepdims=True)
    stiff_high, stiff_low = split(stiffness)
    stiff_all = jnp.concatenate([stiff_high, stiff_high, stiff_low], axis=1)

    def spread(first, second):
        high, low = split(jnp.concatenate([first, second], axis=1))
        cells = jnp.concatenate([high, low, high], axis=0)
        both = jnp.dot(stiff_all, cells, preferred_element_type=F32)
        return both[:, :128], both[:, 128:]

    def local_terms(lumped, inverse, rates, scale, lam_to, diag_to):
        wall = jnp.where(node < SIDE, jnp.broadcast_to(rates, (NODES, 128)), 0.0)
        stiff_part = stiff_diag * scale
        for q in range(modes):
            wave = ((m * modes + q + 1) // 2).astype(F32) * (2.0 / (modes * RING * RING))
            value = (INV_STEP + (wave * wave) * inverse) * lumped + wall
            lam_to[q] = value
            diag_to[q] = stiff_part + value

    local_terms(ones, weights, flow, elem_scale, lam, rate)
    for q in range(modes):
        fld[q] = coeff[pl.ds(q, NODES, stride=modes), :]

    first_nodes = pl.ds(0, SIDE, stride=SIDE)
    last_nodes = pl.ds(SIDE - 1, SIDE, stride=SIDE)
    def turn(value, shift):
        return pltpu.roll(value, shift % 128, 1) if shift % 128 else value

    def join_rows(values, q):
        lower = values[q, 0:SIDE, :]
        upper = values[q, NODES - SIDE : NODES, :]
        values[q, 0:SIDE, :] = lower + jnp.where(row > 0, turn(upper, 1), 0.0)
        values[q, NODES - SIDE : NODES, :] = upper + jnp.where(row < 15, turn(lower, -1), 0.0)

    for pair in range(modes // 2):
        applied = spread(fld[2 * pair], fld[2 * pair + 1])
        for h in range(2):
            q = 2 * pair + h
            res[q] = (INV_STEP * ones - lam[q]) * fld[q] - elem_scale * applied[h]
    quad = lane // 32
    outer = col % 2

    def pack(pieces, send, shift):
        for g in range(len(pieces) // 4):
            total = None
            for k in range(4):
                piece = turn(pieces[4 * g + k], 32 * k + shift)
                total = piece if total is None else jnp.where(quad == k, piece, total)
            send[g] = total

    def join_inner(values):
        for q in range(modes):
            low, high = values[q, first_nodes, :], values[q, last_nodes, :]
            values[q, first_nodes, :] = low + jnp.where(col == 0, 0.0, turn(high, 16))
            values[q, last_nodes, :] = high + jnp.where(col == 7, 0.0, turn(low, -16))

    def join_halo(values, beside, inner, both):
        for g in range(modes // 4):
            left_low, left_high = beside[0, g, first_nodes, :], beside[0, g, last_nodes, :]
            right_low, right_high = beside[1, g, first_nodes, :], beside[1, g, last_nodes, :]
            add_left = turn(left_low, -16)
            add_right = turn(right_high, 16)
            for k in range(4):
                q = 4 * g + k
                low, high = values[q, first_nodes, :], values[q, last_nodes, :]
                near = turn(left_high, -32 * k - 16)
                past = turn(right_low, 112 - 32 * k)
                values[q, first_nodes, :] = jnp.where(col == 0, low + near, low)
                values[q, last_nodes, :] = jnp.where(col == 7, high + past, high)
                if both:
                    add_left = jnp.where(col == 2 * k + 1, turn(low, 32 * k + 16), add_left)
                    add_right = jnp.where(col == 2 * k, turn(high, 32 * k + 16), add_right)
            if both:
                if not inner:
                    add_left = jnp.where(outer == 1, add_left, 0.0)
                    add_right = jnp.where(outer == 0, add_right, 0.0)
                beside[0, g, last_nodes, :] = left_high + add_left
                beside[1, g, first_nodes, :] = right_low + add_right
                if inner:
                    beside[0, g, first_nodes, :] = left_low + jnp.where(
                        outer == 1, turn(left_high, 16), 0.0
                    )
                    beside[1, g, last_nodes, :] = right_high + jnp.where(
                        outer == 0, turn(right_low, -16), 0.0
                    )
        for q in range(modes):
            join_rows(values, q)
        if both:
            for side in range(2):
                for g in range(modes // 4):
                    join_rows(beside.at[side], g)

    for k, d in lots:
        source = (z - d + RING) % RING
        for rr in range(2):
            if rr == 0:
                zcopy[3, d, 0].wait_recv()
            if (d, rr) != (1, 0):
                zcopy[0, d, rr].wait_recv()
            line = zc.at[source, rows[rr]]
            line[112:128, :] = last_node(line[0:16, :], far_ends[source], rr)
            pass_values(k, source, rr, zc.at[source, rows[rr]])

    settle(trait_copies, theirs)
    join_inner(rate)
    side_scale = []
    here = lane >= 64
    for side in range(2):
        def window(mine, others):
            return jnp.where(here == (side == 0), turn(mine, 64), turn(others, 64))

        local_terms(
            window(ones, theirs[side, 0:NODES, :]),
            window(weights, theirs[side, NODES : 2 * NODES, :]),
            window(flow, theirs[side, 2 * NODES + 1 : 2 * NODES + 2, :]),
            window(elem_scale, theirs[side, 2 * NODES : 2 * NODES + 1, :]),
            work,
            inc,
        )
        join_inner(inc)
        for q in range(modes):
            at = first_nodes if side == 0 else last_nodes
            value = turn(inc[q, at, :], 64)
            rate[q, at, :] = jnp.where(col == (0 if side == 0 else 7), value, rate[q, at, :])
            join_rows(inc, q)
            inc[q] = RELAX / inc[q]
        shift = -32 if side == 0 else -64
        pack([work[q] for q in range(modes)], side_lam.at[side], shift)
        pack([inc[q] for q in range(modes)], side_rate.at[side], shift)

        @pl.when(jnp.logical_not(has_left if side == 0 else has_right))
        def _():
            side_rate[side] = jnp.zeros(side_rate.shape[1:], F32)

        scales = window(elem_scale, theirs[side, 2 * NODES : 2 * NODES + 1, :])
        total = None
        for k in range(4):
            piece = turn(scales, 32 * k + shift)
            total = piece if total is None else jnp.where(quad == k, piece, total)
        side_scale.append(total)
    for q in range(modes):
        join_rows(rate, q)
        rate[q] = RELAX / rate[q]

    bcopy = []
    for part in range(2):
        for k, d in lots:
            source = (z - d + RING) % RING
            for rr in range(2):
                zcopy[1 + part, d, rr].wait_recv()
                if part == 1:
                    line = zg.at[source, rows[rr]]
                    line[1, 48:64, :] = last_node(line[0, 0:16, :], far_ends[source], 2 + rr)
                pass_grad(k, source, rr, part, zg.at[source, rows[rr], part])
        if part == 0:
            for copy in later[6:]:
                copy.wait()
        for (what, k, mask), copy in xcopy.items():
            if what == 2 + part or (what < 2 and part == 0):
                copy.wait_recv()
        advect = None
        for kind, src in enumerate((xc, xy, xx)):
            pieces = []
            for h in range(2):
                at = 32 * part + 16 * h
                piece = src[:, part, 16 * h : 16 * h + 16, :] if kind == 1 else src[:, at : at + 16, :]
                pieces.append(piece.reshape(-1, 128))
            which = 0 if kind == 0 else 2
            phys = dot3(tab[which], tab[which + 1], jnp.concatenate(pieces, axis=1))
            speed = jnp.concatenate([vel[kind, 2 * part], vel[kind, 2 * part + 1]], axis=1)
            term = speed.astype(F32) * phys
            advect = term if advect is None else advect + term
        back = dot3(tab[4], tab[5], advect)
        for h in range(2):
            for t in range(RING * RING):
                hat[part, t, 16 * h : 16 * h + 16, :] = back[
                    16 * t : 16 * t + 16, 128 * h : 128 * h + 128
                ]
        mine = pl.ds(pl.multiple_of(m * 64 + 32 * part, 32), 32)
        for d in range(1, RING * RING):
            target = (m + d) % (RING * RING)
            copy = pltpu.make_async_remote_copy(
                src_ref=hat.at[part, target],
                dst_ref=adv.at[mine],
                send_sem=bs.at[part, d - 1],
                recv_sem=br.at[part, d - 1],
                device_id={"mode": target},
                device_id_type=MESH,
            )
            copy.start()
            bcopy.append(copy)
        adv[mine, :] = hat[part, m]
    for copy in bcopy:
        copy.wait_recv()

    for q in range(modes):
        res[q] = res[q] - ones * adv[pl.ds(q, NODES, stride=modes), :]
    join_inner(res)
    for side in range(2):
        pack([res[q] for q in range(modes)], tsend.at[side], 32 * side)
    settle(swap([(tsend.at[0], halo.at[1]), (tsend.at[1], halo.at[0])], 1), halo)
    join_halo(res, halo, False, True)

    for q in range(modes):
        inc[q] = rate[q] * res[q]
    for side in range(2):
        for g in range(modes // 4):
            far[side, g] = side_rate[side, g] * halo[side, g]
    for sweep in range(1, SWEEPS):
        for pair in range(modes // 2):
            applied = spread(inc[2 * pair], inc[2 * pair + 1])
            for h in range(2):
                q = 2 * pair + h
                work[q] = elem_scale * applied[h] + lam[q] * inc[q]
        for side in range(2):
            for pair in range(modes // 8):
                applied = spread(far[side, 2 * pair], far[side, 2 * pair + 1])
                for h in range(2):
                    g = 2 * pair + h
                    beside[side, g] = side_scale[side] * applied[h] + side_lam[side, g] * far[side, g]
        join_inner(work)
        join_halo(work, beside, True, sweep < SWEEPS - 1)
        for q in range(modes):
            total = inc[q] + rate[q] * (res[q] - work[q])
            if sweep < SWEEPS - 1:
                inc[q] = total
            else:
                out[pl.ds(q, NODES, stride=modes), :] = fld[q] + total
        if sweep < SWEEPS - 1:
            for side in range(2):
                for g in range(modes // 4):
                    far[side, g] = far[side, g] + side_rate[side, g] * (
                        halo[side, g] - beside[side, g]
                    )

    for copies in (zcopy, xcopy):
        for copy in copies.values():
            copy.wait_send()
    for copy in bcopy:
        copy.wait_send()


def local(
    tables, coeff, vel_axial, vel_radial, swirl_rate, col_width, row_height, stiffness, stiff_elem,
    mass, azim_weight, wall_flag, transfer,
):
    modes = coeff.shape[1]
    planes = vel_axial.shape[1]
    dma = pltpu.SemaphoreType.DMA
    field = pltpu.VMEM((modes, NODES, 128), F32)
    flat = pltpu.VMEM((NODES * modes, 128), F32)
    columns = pltpu.VMEM((2, modes // 4, NODES, 128), F32)
    rows = pltpu.VMEM((RING, 2, 8 * modes, 128), F32)
    blocks = pltpu.VMEM((RING * RING, 4 * modes, 128), F32)
    halves = pltpu.VMEM((RING * RING, 2, 2 * modes, 128), F32)
    operands = (
        coeff.reshape(NODES * modes, 128),
        swirl_rate,
        vel_radial,
        vel_axial,
        jnp.asarray(tables),
        col_width,
        row_height,
        stiffness,
        stiff_elem.reshape(1, 128),
        mass,
        azim_weight,
        wall_flag,
        transfer,
    )
    result = pl.pallas_call(
        functools.partial(kernel, modes),
        out_shape=pltpu.VMEM((NODES * modes, 128), F32),
        in_specs=[pl.BlockSpec(memory_space=pl.ANY)] * len(operands),
        out_specs=pl.BlockSpec(memory_space=pltpu.VMEM),
        scratch_shapes=[
            flat,
            pltpu.SMEM(col_width.shape, F32),
            pltpu.SMEM(row_height.shape, F32),
            pltpu.VMEM((NODES, NODES), F32),
            pltpu.VMEM((1, 128), F32),
            pltpu.VMEM((2 * NODES + SIDE, 128), F32),
            pltpu.SMEM(wall_flag.shape, jnp.int32),
            pltpu.SMEM(transfer.shape, F32),
            pltpu.VMEM((3, 4, planes, 128), BF16),
            pltpu.VMEM(tables.shape, BF16),
            flat,
            pltpu.VMEM((RING * modes, 128), F32),
            pltpu.VMEM((RING, modes, 128), F32),
            rows,
            pltpu.VMEM((RING, 2, 2, 4 * modes, 128), F32),
            rows,
            blocks,
            blocks,
            halves,
            pltpu.VMEM((2, RING * RING, 2 * modes, 128), F32),
            flat,
            field,
            field,
            field,
            field,
            field,
            field,
            pltpu.VMEM((2, 2 * NODES + SIDE, 128), F32),
            columns,
            columns,
            columns,
            columns,
            columns,
            columns,
            dma((13,)),
            dma((4, 3, 2)),
            dma((4, 3, 2)),
            dma((4, 4, 3)),
            dma((4, 4, 3)),
            dma((2, 15)),
            dma((2, 15)),
            dma((2, 2)),
            dma((2, 2)),
        ],
        compiler_params=pltpu.CompilerParams(collective_id=0, has_side_effects=True),
    )(*operands)
    return result.reshape(coeff.shape)


def solution(mesh):
    tables = fourier_tables(256)
    return jax.shard_map(
        functools.partial(local, tables),
        mesh=mesh,
        in_specs=(
            P(None, "mode", "elem"),
            P("mode", None, "elem"),
            P("mode", None, "elem"),
            P("mode", None, "elem"),
            P("elem"),
            P(),
            P(),
            P("elem"),
            P(None, "elem"),
            P(None, "elem"),
            P("elem"),
            P("elem"),
        ),
        out_specs=P(None, "mode", "elem"),
        check_vma=False,
    )
```

```python
import functools

import jax
import jax.numpy as jnp
import ml_dtypes
import numpy as np
from jax import lax
from jax.experimental import pallas as pl
from jax.experimental.pallas import tpu as pltpu
from jax.sharding import PartitionSpec as P

MESH = pl.DeviceIdType.MESH
SIDE = 8
NODES = 64
SWEEPS = 3
INV_STEP = 2.0
RELAX = 0.8
RING = 4
F32 = jnp.float32
BF16 = jnp.bfloat16


def cheb_matrix(side_count):
    points = np.cos(np.pi * np.arange(side_count) / (side_count - 1))
    weights = np.ones(side_count)
    weights[0] = weights[-1] = 2.0
    weights = weights * (-1.0) ** np.arange(side_count)
    table = np.zeros((side_count, side_count))
    for row in range(side_count):
        for col in range(side_count):
            if row != col:
                table[row, col] = weights[row] / weights[col] / (points[row] - points[col])
        table[row, row] = -np.sum(table[row])
    return table


def split_table(table):
    high = table.astype(np.float32).astype(ml_dtypes.bfloat16)
    low = (table - high.astype(np.float64)).astype(np.float32).astype(ml_dtypes.bfloat16)
    return [high, low]


def fourier_tables(planes):
    q = np.arange(planes)
    k = (q + 1) // 2
    angle = 2.0 * np.pi / planes * ((k[:, None] * np.arange(planes)[None, :]) % planes)
    sine = ((q % 2 == 0) & (q > 0))[:, None]
    wave = k[:, None].astype(np.float64)
    basis = np.where(sine, np.sin(angle), np.cos(angle))
    slope = np.where(sine, wave * np.cos(angle), -wave * np.sin(angle))
    norm = np.where((q == 0) | (q == planes - 1), 1.0, 2.0) / planes
    forward = basis * norm[:, None]
    return np.stack(split_table(slope.T) + split_table(basis.T) + split_table(forward))


def split(value):
    high = value.astype(BF16)
    return high, (value - high.astype(F32)).astype(BF16)


def dot3(tab_high, tab_low, value):
    high, low = split(value)
    total = jnp.dot(tab_high, high, preferred_element_type=F32)
    total += jnp.dot(tab_high, low, preferred_element_type=F32)
    return total + jnp.dot(tab_low, high, preferred_element_type=F32)


def kernel(
    modes, coeff_in, vel_t, vel_y, vel_x, tables, width_in, height_in, stiff_in, elem_in, mass_in,
    azim_in, flag_in, transfer_in, out,
    coeff, col_width, row_height, stiff, stiff_elem, traits, wall_flag, transfer,
    vel, tab, grad_y, ends, far_ends, zc, zg, zx, xc, xx, xy, partial, hat, adv, fld, lam, rate, res, inc, work,
    theirs, side_lam, side_rate, tsend, halo, far, beside, local_sem, zs, zr, xs, xr, bs, br, hs, hr,
):
    s, m = lax.axis_index("elem"), lax.axis_index("mode")
    elems = lax.axis_size("elem")
    z, x = m // RING, m % RING
    cheb = cheb_matrix(SIDE)

    left, right = lax.max(s - 1, 0), lax.min(s + 1, elems - 1)
    has_left, has_right = s > 0, s < elems - 1
    barrier = pltpu.get_barrier_semaphore()
    for step in range(1, RING):
        if step != 2:
            pl.semaphore_signal(
                barrier,
                inc=1,
                device_id={"mode": (z + step) % RING * RING + x},
                device_id_type=MESH,
            )
        pl.semaphore_signal(
            barrier, inc=1, device_id={"mode": z * RING + (x + step) % RING}, device_id_type=MESH
        )
    for other, there in ((left, has_left), (right, has_right)):

        @pl.when(there)
        def _():
            pl.semaphore_signal(barrier, inc=1, device_id={"elem": other}, device_id_type=MESH)


    def fetch(pairs):
        copies = [
            pltpu.make_async_copy(src, dst, local_sem.at[i]) for i, (src, dst) in pairs
        ]
        for copy in copies:
            copy.start()
        return copies

    early = fetch(
        enumerate([(coeff_in, coeff), (height_in, row_height), (width_in, col_width)])
    )
    later = fetch(
        enumerate(
            [
                (stiff_in, stiff),
                (elem_in, stiff_elem),
                (mass_in, traits.at[pl.ds(0, NODES)]),
                (azim_in, traits.at[pl.ds(NODES, NODES)]),
                (flag_in, wall_flag),
                (transfer_in, transfer),
                (vel_t, vel.at[0]),
                (vel_y, vel.at[1]),
                (vel_x, vel.at[2]),
                (tables, tab),
            ],
            3,
        )
    )
    for copy in early:
        copy.wait()

    lane = lax.broadcasted_iota(jnp.int32, (1, 128), 1)
    col, row = lane // 16, lane % 16
    width = jnp.zeros((1, 128), F32)
    for a in range(8):
        width = jnp.where(col == a, col_width[a], width)
    height = jnp.zeros((1, 128), F32)
    for b in range(16):
        height = jnp.where(row == b, row_height[b], height)
    scale_x = 2.0 / width
    scale_y = 2.0 / height

    @pl.loop(0, SIDE)
    def _(i):
        start = pl.multiple_of(i * 16, 16)
        cells = [coeff[pl.ds(start + j * 128, 16), :] for j in range(SIDE)]
        place = pl.multiple_of(i % 4 // 2 * 64 + i // 4 * 32 + i % 2 * 16, 16)
        for j in range(SIDE):
            total = cheb[j, 0] * cells[0]
            for k in range(1, SIDE):
                total += cheb[j, k] * cells[k]
            grad_y[pl.ds(place + j * 128, 16), :] = total * scale_y

    own_row = x // 2
    rows = (1 - own_row, own_row)
    for plane in range(RING):
        tile = jnp.zeros((16, 128), F32)
        for kind, src in ((0, coeff), (1, grad_y)):
            for rr in range(2):
                at = pl.multiple_of((2 * plane + rows[rr]) * 128 + 112, 16)
                edge = pltpu.roll(src[pl.ds(at, 16), :], 32 * kind + 16 * rr + 16, 1)
                tile = jnp.where(col == 2 * kind + rr, edge, tile)
        ends[16 * plane : 16 * plane + 16, :] = tile

    def last_node(first, tile, which):
        return jnp.where(
            lane < 112, pltpu.roll(first, 112, 1), pltpu.roll(tile, 112 - 16 * which, 1)
        )

    pl.semaphore_wait(
        barrier, 2 * RING - 3 + has_left.astype(jnp.int32) + has_right.astype(jnp.int32)
    )

    zcopy, xcopy = {}, {}
    near = [(rr, d) for rr in range(2) for d in (1, 3)]
    waves = near + [(rr, 2) for rr in range(2)]
    lots = ((1, 1), (2, 3), (3, 2))

    def row_start(plane, rr):
        return (plane * 2 + rows[rr]) * 128

    def start_z(what, d, rr, src, dst):
        copy = pltpu.make_async_remote_copy(
            src_ref=src,
            dst_ref=dst,
            send_sem=zs.at[what, d - 1, rr],
            recv_sem=zr.at[what, d - 1, rr],
            device_id={"mode": (z + d) % RING * RING + x},
            device_id_type=MESH,
        )
        copy.start()
        zcopy[what, d, rr] = copy

    def swap(pairs, turn_id):
        copies = []
        for side, other, there in ((0, left, has_left), (1, right, has_right)):
            copy = pltpu.make_async_remote_copy(
                src_ref=pairs[side][0],
                dst_ref=pairs[side][1],
                send_sem=hs.at[turn_id, side],
                recv_sem=hr.at[turn_id, 1 - side],
                device_id={"elem": other},
                device_id_type=MESH,
            )
            pl.when(there)(copy.start)
            copies.append(copy)
        return copies

    def settle(copies, theirs):
        for side, there in ((0, has_left), (1, has_right)):

            @pl.when(there)
            def _():
                copies[side].wait_send()
                copies[1 - side].wait_recv()

            @pl.when(jnp.logical_not(there))
            def _():
                theirs[side] = jnp.zeros(theirs.shape[1:], F32)

    for copy in later[:6]:
        copy.wait()
    flow = jnp.zeros((1, 128), F32)
    for a in range(8):
        flow = jnp.where(col == a, wall_flag[a].astype(F32) * transfer[a], flow)
    flow = jnp.where(row == 0, flow, 0.0)
    elem_scale = stiff_elem[...]
    line8 = lax.broadcasted_iota(jnp.int32, (SIDE, 128), 0)
    traits[2 * NODES : 2 * NODES + SIDE, :] = jnp.where(line8 == 0, elem_scale, flow)
    trait_copies = swap([(traits, theirs.at[1]), (traits, theirs.at[0])], 0)

    def send_values(d, rr):
        if rr == 0:
            at = pl.ds(pl.multiple_of((z + d) % RING * 16, 16), 16)
            start_z(3, d, 0, ends.at[at], far_ends.at[z])
        at = pl.ds(pl.multiple_of(row_start((z + d) % RING, rr), 128), 112)
        start_z(0, d, rr, coeff.at[at], zc.at[z, rows[rr], pl.ds(0, 112)])

    for rr, d in near:
        send_values(d, rr)

    partner = {1: x + 1 - 2 * (x % 2), 2: (x + 2) % RING, 3: RING - 1 - x}

    def start_x(what, k, mask, src, dst):
        copy = pltpu.make_async_remote_copy(
            src_ref=src,
            dst_ref=dst,
            send_sem=xs.at[what, k, mask - 1],
            recv_sem=xr.at[what, k, mask - 1],
            device_id={"mode": z * RING + partner[mask]},
            device_id_type=MESH,
        )
        copy.start()
        xcopy[what, k, mask] = copy

    def half(target, size):
        return pl.ds(pl.multiple_of(target % 2 * size, size), size)

    def pass_values(k, source, rr, line):
        cells = [line[16 * i : 16 * i + 16, :] for i in range(SIDE)]
        slopes = zx.at[source, rows[rr]]
        for i in range(SIDE):
            total = cheb[i, 0] * cells[0]
            for j in range(1, SIDE):
                total += cheb[i, j] * cells[j]
            slopes[16 * i : 16 * i + 16, :] = total * scale_x
        spot = source * RING + x
        for what, src, dst in ((0, line, xc), (1, slopes, xx)):
            for mask in (2, 3) if rr == 0 else (1,):
                start_x(what, k, mask, src.at[half(partner[mask], 64)], dst.at[spot])
            if rr == 1:
                dst[spot] = src[half(x, 64), :]

    def pass_grad(k, source, rr, part, line):
        spot = source * RING + x
        for mask in (2, 3) if rr == 0 else (1,):
            start_x(2 + part, k, mask, line.at[half(partner[mask], 32)], xy.at[spot, part])
        if rr == 1:
            xy[spot, part] = line[half(x, 32), :]

    for rr in range(2):
        at = pl.multiple_of(row_start(z, rr), 128)
        pass_values(0, z, rr, coeff.at[pl.ds(at, 128)])
        for part in range(2):
            pass_grad(0, z, rr, part, grad_y.at[pl.ds(at + 64 * part, 64)])

    zcopy[0, 1, 0].wait_recv()
    for rr in range(2):
        send_values(2, rr)
    for part, size in ((0, 64), (1, 48)):
        for rr, d in waves[4:] + waves[:4]:
            at = pl.ds(pl.multiple_of(row_start((z + d) % RING, rr) + 64 * part, 64), size)
            start_z(1 + part, d, rr, grad_y.at[at], zg.at[z, rows[rr], part, pl.ds(0, size)])

    ones = traits[0:NODES, :]
    weights = traits[NODES : 2 * NODES, :]
    node = lax.broadcasted_iota(jnp.int32, (NODES, 128), 0)
    stiffness = stiff[...]
    on_diag = lax.broadcasted_iota(jnp.int32, (NODES, NODES), 0) == lax.broadcasted_iota(
        jnp.int32, (NODES, NODES), 1
    )
    stiff_diag = jnp.sum(jnp.where(on_diag, stiffness, 0.0), axis=1, keepdims=True)
    stiff_high, stiff_low = split(stiffness)
    stiff_all = jnp.concatenate([stiff_high, stiff_high, stiff_low], axis=1)

    def spread(first, second):
        high, low = split(jnp.concatenate([first, second], axis=1))
        cells = jnp.concatenate([high, low, high], axis=0)
        both = jnp.dot(stiff_all, cells, preferred_element_type=F32)
        return both[:, :128], both[:, 128:]

    def local_terms(lumped, inverse, rates, scale, lam_to, diag_to):
        wall = jnp.where(node < SIDE, jnp.broadcast_to(rates, (NODES, 128)), 0.0)
        stiff_part = stiff_diag * scale
        for q in range(modes):
            wave = ((m * modes + q + 1) // 2).astype(F32) * (2.0 / (modes * RING * RING))
            value = (INV_STEP + (wave * wave) * inverse) * lumped + wall
            lam_to[q] = value
            diag_to[q] = stiff_part + value

    local_terms(ones, weights, flow, elem_scale, lam, rate)
    for q in range(modes):
        fld[q] = coeff[pl.ds(q, NODES, stride=modes), :]

    first_nodes = pl.ds(0, SIDE, stride=SIDE)
    last_nodes = pl.ds(SIDE - 1, SIDE, stride=SIDE)
    def turn(value, shift):
        return pltpu.roll(value, shift % 128, 1) if shift % 128 else value

    def join_rows(values, q):
        lower = values[q, 0:SIDE, :]
        upper = values[q, NODES - SIDE : NODES, :]
        values[q, 0:SIDE, :] = lower + jnp.where(row > 0, turn(upper, 1), 0.0)
        values[q, NODES - SIDE : NODES, :] = upper + jnp.where(row < 15, turn(lower, -1), 0.0)

    for pair in range(modes // 2):
        applied = spread(fld[2 * pair], fld[2 * pair + 1])
        for h in range(2):
            q = 2 * pair + h
            res[q] = (INV_STEP * ones - lam[q]) * fld[q] - elem_scale * applied[h]
    quad = lane // 32
    outer = col % 2

    def pack(pieces, send, shift):
        for g in range(len(pieces) // 4):
            total = None
            for k in range(4):
                piece = turn(pieces[4 * g + k], 32 * k + shift)
                total = piece if total is None else jnp.where(quad == k, piece, total)
            send[g] = total

    def join_inner(values):
        for q in range(modes):
            low, high = values[q, first_nodes, :], values[q, last_nodes, :]
            values[q, first_nodes, :] = low + jnp.where(col == 0, 0.0, turn(high, 16))
            values[q, last_nodes, :] = high + jnp.where(col == 7, 0.0, turn(low, -16))

    def join_halo(values, beside, inner, both):
        for g in range(modes // 4):
            left_low, left_high = beside[0, g, first_nodes, :], beside[0, g, last_nodes, :]
            right_low, right_high = beside[1, g, first_nodes, :], beside[1, g, last_nodes, :]
            add_left = turn(left_low, -16)
            add_right = turn(right_high, 16)
            for k in range(4):
                q = 4 * g + k
                low, high = values[q, first_nodes, :], values[q, last_nodes, :]
                near = turn(left_high, -32 * k - 16)
                past = turn(right_low, 112 - 32 * k)
                values[q, first_nodes, :] = jnp.where(col == 0, low + near, low)
                values[q, last_nodes, :] = jnp.where(col == 7, high + past, high)
                if both:
                    add_left = jnp.where(col == 2 * k + 1, turn(low, 32 * k + 16), add_left)
                    add_right = jnp.where(col == 2 * k, turn(high, 32 * k + 16), add_right)
            if both:
                if not inner:
                    add_left = jnp.where(outer == 1, add_left, 0.0)
                    add_right = jnp.where(outer == 0, add_right, 0.0)
                beside[0, g, last_nodes, :] = left_high + add_left
                beside[1, g, first_nodes, :] = right_low + add_right
                if inner:
                    beside[0, g, first_nodes, :] = left_low + jnp.where(
                        outer == 1, turn(left_high, 16), 0.0
                    )
                    beside[1, g, last_nodes, :] = right_high + jnp.where(
                        outer == 0, turn(right_low, -16), 0.0
                    )
        for q in range(modes):
            join_rows(values, q)
        if both:
            for side in range(2):
                for g in range(modes // 4):
                    join_rows(beside.at[side], g)

    for k, d in lots:
        source = (z - d + RING) % RING
        for rr in range(2):
            if rr == 0:
                zcopy[3, d, 0].wait_recv()
            if (d, rr) != (1, 0):
                zcopy[0, d, rr].wait_recv()
            line = zc.at[source, rows[rr]]
            line[112:128, :] = last_node(line[0:16, :], far_ends[source], rr)
            pass_values(k, source, rr, zc.at[source, rows[rr]])

    settle(trait_copies, theirs)
    join_inner(rate)
    side_scale = []
    here = lane >= 64
    for side in range(2):
        def window(mine, others):
            return jnp.where(here == (side == 0), turn(mine, 64), turn(others, 64))

        local_terms(
            window(ones, theirs[side, 0:NODES, :]),
            window(weights, theirs[side, NODES : 2 * NODES, :]),
            window(flow, theirs[side, 2 * NODES + 1 : 2 * NODES + 2, :]),
            window(elem_scale, theirs[side, 2 * NODES : 2 * NODES + 1, :]),
            work,
            inc,
        )
        join_inner(inc)
        for q in range(modes):
            at = first_nodes if side == 0 else last_nodes
            value = turn(inc[q, at, :], 64)
            rate[q, at, :] = jnp.where(col == (0 if side == 0 else 7), value, rate[q, at, :])
            join_rows(inc, q)
            inc[q] = RELAX / inc[q]
        shift = -32 if side == 0 else -64
        pack([work[q] for q in range(modes)], side_lam.at[side], shift)
        pack([inc[q] for q in range(modes)], side_rate.at[side], shift)

        @pl.when(jnp.logical_not(has_left if side == 0 else has_right))
        def _():
            side_rate[side] = jnp.zeros(side_rate.shape[1:], F32)

        scales = window(elem_scale, theirs[side, 2 * NODES : 2 * NODES + 1, :])
        total = None
        for k in range(4):
            piece = turn(scales, 32 * k + shift)
            total = piece if total is None else jnp.where(quad == k, piece, total)
        side_scale.append(total)
    for q in range(modes):
        join_rows(rate, q)
        rate[q] = RELAX / rate[q]

    order = [(2, dx) for dx in (2, 1, 3, 0)]
    order += [(dz, dx) for dx in (2, 1, 3, 0) for dz in (1, 3)] + [(0, dx) for dx in (2, 1, 3)]
    bcopy = []
    for part in range(2):
        for k, d in lots:
            source = (z - d + RING) % RING
            for rr in range(2):
                zcopy[1 + part, d, rr].wait_recv()
                if part == 1:
                    line = zg.at[source, rows[rr]]
                    line[1, 48:64, :] = last_node(line[0, 0:16, :], far_ends[source], 2 + rr)
                pass_grad(k, source, rr, part, zg.at[source, rows[rr], part])
        if part == 0:
            for copy in later[6:]:
                copy.wait()
        if part == 0:
            for (what, k, mask), copy in xcopy.items():
                if what < 2:
                    copy.wait_recv()

        def advection(kind, src):
            pieces = []
            for h in range(2):
                at = 32 * part + 16 * h
                piece = src[:, part, 16 * h : 16 * h + 16, :] if kind == 1 else src[:, at : at + 16, :]
                pieces.append(piece.reshape(-1, 128))
            which = 0 if kind == 0 else 2
            phys = dot3(tab[which], tab[which + 1], jnp.concatenate(pieces, axis=1))
            speed = jnp.concatenate([vel[kind, 2 * part], vel[kind, 2 * part + 1]], axis=1)
            return speed.astype(F32) * phys

        partial[...] = advection(0, xc) + advection(2, xx)
        for (what, k, mask), copy in xcopy.items():
            if what == 2 + part:
                copy.wait_recv()
        advect = partial[...] + advection(1, xy)
        back = dot3(tab[4], tab[5], advect)
        for h in range(2):
            for t in range(RING * RING):
                hat[part, t, 16 * h : 16 * h + 16, :] = back[
                    16 * t : 16 * t + 16, 128 * h : 128 * h + 128
                ]
        mine = pl.ds(pl.multiple_of(m * 64 + 32 * part, 32), 32)
        for d, (dz, dx) in enumerate(order, 1):
            target = (z + dz) % RING * RING + (x + dx) % RING
            copy = pltpu.make_async_remote_copy(
                src_ref=hat.at[part, target],
                dst_ref=adv.at[mine],
                send_sem=bs.at[part, d - 1],
                recv_sem=br.at[part, d - 1],
                device_id={"mode": target},
                device_id_type=MESH,
            )
            copy.start()
            bcopy.append(copy)
        adv[mine, :] = hat[part, m]
    for copy in bcopy:
        copy.wait_recv()

    for q in range(modes):
        res[q] = res[q] - ones * adv[pl.ds(q, NODES, stride=modes), :]
    join_inner(res)
    for side in range(2):
        pack([res[q] for q in range(modes)], tsend.at[side], 32 * side)
    settle(swap([(tsend.at[0], halo.at[1]), (tsend.at[1], halo.at[0])], 1), halo)
    join_halo(res, halo, False, True)

    for q in range(modes):
        inc[q] = rate[q] * res[q]
    for side in range(2):
        for g in range(modes // 4):
            far[side, g] = side_rate[side, g] * halo[side, g]
    for sweep in range(1, SWEEPS):
        for pair in range(modes // 2):
            applied = spread(inc[2 * pair], inc[2 * pair + 1])
            for h in range(2):
                q = 2 * pair + h
                work[q] = elem_scale * applied[h] + lam[q] * inc[q]
        for side in range(2):
            for pair in range(modes // 8):
                applied = spread(far[side, 2 * pair], far[side, 2 * pair + 1])
                for h in range(2):
                    g = 2 * pair + h
                    beside[side, g] = side_scale[side] * applied[h] + side_lam[side, g] * far[side, g]
        join_inner(work)
        join_halo(work, beside, True, sweep < SWEEPS - 1)
        for q in range(modes):
            total = inc[q] + rate[q] * (res[q] - work[q])
            if sweep < SWEEPS - 1:
                inc[q] = total
            else:
                out[pl.ds(q, NODES, stride=modes), :] = fld[q] + total
        if sweep < SWEEPS - 1:
            for side in range(2):
                for g in range(modes // 4):
                    far[side, g] = far[side, g] + side_rate[side, g] * (
                        halo[side, g] - beside[side, g]
                    )

    for copies in (zcopy, xcopy):
        for copy in copies.values():
            copy.wait_send()
    for copy in bcopy:
        copy.wait_send()


def local(
    tables, coeff, vel_axial, vel_radial, swirl_rate, col_width, row_height, stiffness, stiff_elem,
    mass, azim_weight, wall_flag, transfer,
):
    modes = coeff.shape[1]
    planes = vel_axial.shape[1]
    dma = pltpu.SemaphoreType.DMA
    field = pltpu.VMEM((modes, NODES, 128), F32)
    flat = pltpu.VMEM((NODES * modes, 128), F32)
    columns = pltpu.VMEM((2, modes // 4, NODES, 128), F32)
    rows = pltpu.VMEM((RING, 2, 8 * modes, 128), F32)
    blocks = pltpu.VMEM((RING * RING, 4 * modes, 128), F32)
    halves = pltpu.VMEM((RING * RING, 2, 2 * modes, 128), F32)
    operands = (
        coeff.reshape(NODES * modes, 128),
        swirl_rate,
        vel_radial,
        vel_axial,
        jnp.asarray(tables),
        col_width,
        row_height,
        stiffness,
        stiff_elem.reshape(1, 128),
        mass,
        azim_weight,
        wall_flag,
        transfer,
    )
    result = pl.pallas_call(
        functools.partial(kernel, modes),
        out_shape=pltpu.VMEM((NODES * modes, 128), F32),
        in_specs=[pl.BlockSpec(memory_space=pl.ANY)] * len(operands),
        out_specs=pl.BlockSpec(memory_space=pltpu.VMEM),
        scratch_shapes=[
            flat,
            pltpu.SMEM(col_width.shape, F32),
            pltpu.SMEM(row_height.shape, F32),
            pltpu.VMEM((NODES, NODES), F32),
            pltpu.VMEM((1, 128), F32),
            pltpu.VMEM((2 * NODES + SIDE, 128), F32),
            pltpu.SMEM(wall_flag.shape, jnp.int32),
            pltpu.SMEM(transfer.shape, F32),
            pltpu.VMEM((3, 4, planes, 128), BF16),
            pltpu.VMEM(tables.shape, BF16),
            flat,
            pltpu.VMEM((RING * modes, 128), F32),
            pltpu.VMEM((RING, modes, 128), F32),
            rows,
            pltpu.VMEM((RING, 2, 2, 4 * modes, 128), F32),
            rows,
            blocks,
            blocks,
            halves,
            pltpu.VMEM((planes, 256), F32),
            pltpu.VMEM((2, RING * RING, 2 * modes, 128), F32),
            flat,
            field,
            field,
            field,
            field,
            field,
            field,
            pltpu.VMEM((2, 2 * NODES + SIDE, 128), F32),
            columns,
            columns,
            columns,
            columns,
            columns,
            columns,
            dma((13,)),
            dma((4, 3, 2)),
            dma((4, 3, 2)),
            dma((4, 4, 3)),
            dma((4, 4, 3)),
            dma((2, 15)),
            dma((2, 15)),
            dma((2, 2)),
            dma((2, 2)),
        ],
        compiler_params=pltpu.CompilerParams(collective_id=0, has_side_effects=True),
    )(*operands)
    return result.reshape(coeff.shape)


def solution(mesh):
    tables = fourier_tables(256)
    return jax.shard_map(
        functools.partial(local, tables),
        mesh=mesh,
        in_specs=(
            P(None, "mode", "elem"),
            P("mode", None, "elem"),
            P("mode", None, "elem"),
            P("mode", None, "elem"),
            P("elem"),
            P(),
            P(),
            P("elem"),
            P(None, "elem"),
            P(None, "elem"),
            P("elem"),
            P("elem"),
        ),
        out_specs=P(None, "mode", "elem"),
        check_vma=False,
    )
```

```python
import functools

import jax
import jax.numpy as jnp
import ml_dtypes
import numpy as np
from jax import lax
from jax.experimental import pallas as pl
from jax.experimental.pallas import tpu as pltpu
from jax.sharding import PartitionSpec as P

MESH = pl.DeviceIdType.MESH
SIDE = 8
NODES = 64
SWEEPS = 3
INV_STEP = 2.0
RELAX = 0.8
RING = 4
F32 = jnp.float32
BF16 = jnp.bfloat16


def cheb_matrix(side_count):
    points = np.cos(np.pi * np.arange(side_count) / (side_count - 1))
    weights = np.ones(side_count)
    weights[0] = weights[-1] = 2.0
    weights = weights * (-1.0) ** np.arange(side_count)
    table = np.zeros((side_count, side_count))
    for row in range(side_count):
        for col in range(side_count):
            if row != col:
                table[row, col] = weights[row] / weights[col] / (points[row] - points[col])
        table[row, row] = -np.sum(table[row])
    return table


def split_table(table):
    high = table.astype(np.float32).astype(ml_dtypes.bfloat16)
    low = (table - high.astype(np.float64)).astype(np.float32).astype(ml_dtypes.bfloat16)
    return [high, low]


def fourier_tables(planes):
    q = np.arange(planes)
    k = (q + 1) // 2
    angle = 2.0 * np.pi / planes * ((k[:, None] * np.arange(planes)[None, :]) % planes)
    sine = ((q % 2 == 0) & (q > 0))[:, None]
    wave = k[:, None].astype(np.float64)
    basis = np.where(sine, np.sin(angle), np.cos(angle))
    slope = np.where(sine, wave * np.cos(angle), -wave * np.sin(angle))
    norm = np.where((q == 0) | (q == planes - 1), 1.0, 2.0) / planes
    forward = basis * norm[:, None]
    return np.stack(split_table(slope.T) + split_table(basis.T) + split_table(forward))


def split(value):
    high = value.astype(BF16)
    return high, (value - high.astype(F32)).astype(BF16)


def dot3(tab_high, tab_low, value):
    high, low = split(value)
    total = jnp.dot(tab_high, high, preferred_element_type=F32)
    total += jnp.dot(tab_high, low, preferred_element_type=F32)
    return total + jnp.dot(tab_low, high, preferred_element_type=F32)


def kernel(
    modes, coeff_in, vel_t, vel_y, vel_x, tables, width_in, height_in, stiff_in, elem_in, mass_in,
    azim_in, flag_in, transfer_in, out,
    coeff, col_width, row_height, stiff, stiff_elem, traits, wall_flag, transfer,
    vel, tab, grad_y, ends, far_ends, zc, zg, zx, xc, xx, xy, partial, hat, adv, fld, lam, rate, res, inc, work,
    theirs, side_lam, side_rate, tsend, halo, far, beside, local_sem, zs, zr, xs, xr, gs, gr, bs, br, hs, hr,
):
    s, m = lax.axis_index("elem"), lax.axis_index("mode")
    elems = lax.axis_size("elem")
    z, x = m // RING, m % RING
    cheb = cheb_matrix(SIDE)

    left, right = lax.max(s - 1, 0), lax.min(s + 1, elems - 1)
    has_left, has_right = s > 0, s < elems - 1
    barrier = pltpu.get_barrier_semaphore()
    for step in range(1, RING):
        if step != 2:
            pl.semaphore_signal(
                barrier,
                inc=1,
                device_id={"mode": (z + step) % RING * RING + x},
                device_id_type=MESH,
            )
        pl.semaphore_signal(
            barrier, inc=1, device_id={"mode": z * RING + (x + step) % RING}, device_id_type=MESH
        )
    for other, there in ((left, has_left), (right, has_right)):

        @pl.when(there)
        def _():
            pl.semaphore_signal(barrier, inc=1, device_id={"elem": other}, device_id_type=MESH)


    def fetch(pairs):
        copies = [
            pltpu.make_async_copy(src, dst, local_sem.at[i]) for i, (src, dst) in pairs
        ]
        for copy in copies:
            copy.start()
        return copies

    early = fetch(
        enumerate([(coeff_in, coeff), (height_in, row_height), (width_in, col_width)])
    )
    later = fetch(
        enumerate(
            [
                (stiff_in, stiff),
                (elem_in, stiff_elem),
                (mass_in, traits.at[pl.ds(0, NODES)]),
                (azim_in, traits.at[pl.ds(NODES, NODES)]),
                (flag_in, wall_flag),
                (transfer_in, transfer),
                (vel_t, vel.at[0]),
                (vel_y, vel.at[1]),
                (vel_x, vel.at[2]),
                (tables, tab),
            ],
            3,
        )
    )
    for copy in early:
        copy.wait()

    lane = lax.broadcasted_iota(jnp.int32, (1, 128), 1)
    col, row = lane // 16, lane % 16
    width = jnp.zeros((1, 128), F32)
    for a in range(8):
        width = jnp.where(col == a, col_width[a], width)
    height = jnp.zeros((1, 128), F32)
    for b in range(16):
        height = jnp.where(row == b, row_height[b], height)
    scale_x = 2.0 / width
    scale_y = 2.0 / height

    @pl.loop(0, SIDE)
    def _(i):
        start = pl.multiple_of(i * 16, 16)
        cells = [coeff[pl.ds(start + j * 128, 16), :] for j in range(SIDE)]
        later_pair = ((i // 2 + 1) // 2 + 1) % 2
        place = pl.multiple_of(later_pair * 64 + i // 4 * 32 + i % 2 * 16, 16)
        for j in range(SIDE):
            total = cheb[j, 0] * cells[0]
            for k in range(1, SIDE):
                total += cheb[j, k] * cells[k]
            grad_y[pl.ds(place + j * 128, 16), :] = total * scale_y

    own_row = x // 2
    rows = (1 - own_row, own_row)
    for plane in range(RING):
        tile = jnp.zeros((16, 128), F32)
        for kind, src in ((0, coeff), (1, grad_y)):
            for rr in range(2):
                at = pl.multiple_of((2 * plane + rows[rr]) * 128 + 112, 16)
                edge = pltpu.roll(src[pl.ds(at, 16), :], 32 * kind + 16 * rr + 16, 1)
                tile = jnp.where(col == 2 * kind + rr, edge, tile)
        ends[16 * plane : 16 * plane + 16, :] = tile

    def last_node(first, tile, which):
        return jnp.where(
            lane < 112, pltpu.roll(first, 112, 1), pltpu.roll(tile, 112 - 16 * which, 1)
        )

    pl.semaphore_wait(
        barrier, 2 * RING - 3 + has_left.astype(jnp.int32) + has_right.astype(jnp.int32)
    )

    zcopy, xcopy = {}, {}
    near = [(rr, d) for rr in range(2) for d in (1, 3)]
    waves = near + [(rr, 2) for rr in range(2)]
    lots = ((1, 1), (2, 3), (3, 2))

    def row_start(plane, rr):
        return (plane * 2 + rows[rr]) * 128

    def start_z(what, d, rr, src, dst):
        copy = pltpu.make_async_remote_copy(
            src_ref=src,
            dst_ref=dst,
            send_sem=zs.at[what, d - 1, rr],
            recv_sem=zr.at[what, d - 1, rr],
            device_id={"mode": (z + d) % RING * RING + x},
            device_id_type=MESH,
        )
        copy.start()
        zcopy[what, d, rr] = copy

    def swap(pairs, turn_id):
        copies = []
        for side, other, there in ((0, left, has_left), (1, right, has_right)):
            copy = pltpu.make_async_remote_copy(
                src_ref=pairs[side][0],
                dst_ref=pairs[side][1],
                send_sem=hs.at[turn_id, side],
                recv_sem=hr.at[turn_id, 1 - side],
                device_id={"elem": other},
                device_id_type=MESH,
            )
            pl.when(there)(copy.start)
            copies.append(copy)
        return copies

    def settle(copies, theirs):
        for side, there in ((0, has_left), (1, has_right)):

            @pl.when(there)
            def _():
                copies[side].wait_send()
                copies[1 - side].wait_recv()

            @pl.when(jnp.logical_not(there))
            def _():
                theirs[side] = jnp.zeros(theirs.shape[1:], F32)

    for copy in later[:6]:
        copy.wait()
    flow = jnp.zeros((1, 128), F32)
    for a in range(8):
        flow = jnp.where(col == a, wall_flag[a].astype(F32) * transfer[a], flow)
    flow = jnp.where(row == 0, flow, 0.0)
    elem_scale = stiff_elem[...]
    line8 = lax.broadcasted_iota(jnp.int32, (SIDE, 128), 0)
    traits[2 * NODES : 2 * NODES + SIDE, :] = jnp.where(line8 == 0, elem_scale, flow)
    trait_copies = swap([(traits, theirs.at[1]), (traits, theirs.at[0])], 0)

    def send_values(d, rr):
        if rr == 0:
            at = pl.ds(pl.multiple_of((z + d) % RING * 16, 16), 16)
            start_z(3, d, 0, ends.at[at], far_ends.at[z])
        at = pl.ds(pl.multiple_of(row_start((z + d) % RING, rr), 128), 112)
        start_z(0, d, rr, coeff.at[at], zc.at[z, rows[rr], pl.ds(0, 112)])

    for rr, d in near:
        send_values(d, rr)

    order = [(2, dx) for dx in (2, 1, 3, 0)]
    order += [(dz, dx) for dx in (2, 1, 3, 0) for dz in (1, 3)] + [(0, dx) for dx in (2, 1, 3)]
    gcopy = []

    def first_pair(plane, place):
        return pl.ds(
            pl.multiple_of((plane * 2 + place // 2) * 128 + place % 2 * 32, 32), 32
        )

    def send_first_pairs():
        for d, (dz, dx) in enumerate(order):
            plane, place = (z + dz) % RING, (x + dx) % RING
            copy = pltpu.make_async_remote_copy(
                src_ref=grad_y.at[first_pair(plane, place)],
                dst_ref=xy.at[m, 0],
                send_sem=gs.at[d],
                recv_sem=gr.at[d],
                device_id={"mode": plane * RING + place},
                device_id_type=MESH,
            )
            copy.start()
            gcopy.append(copy)
        xy[m, 0] = grad_y[first_pair(z, x), :]

    partner = {1: x + 1 - 2 * (x % 2), 2: (x + 2) % RING, 3: RING - 1 - x}

    def start_x(what, k, mask, src, dst):
        copy = pltpu.make_async_remote_copy(
            src_ref=src,
            dst_ref=dst,
            send_sem=xs.at[what, k, mask - 1],
            recv_sem=xr.at[what, k, mask - 1],
            device_id={"mode": z * RING + partner[mask]},
            device_id_type=MESH,
        )
        copy.start()
        xcopy[what, k, mask] = copy

    def half(target, size):
        return pl.ds(pl.multiple_of(target % 2 * size, size), size)

    def pass_values(k, source, rr, line):
        cells = [line[16 * i : 16 * i + 16, :] for i in range(SIDE)]
        slopes = zx.at[source, rows[rr]]
        for i in range(SIDE):
            total = cheb[i, 0] * cells[0]
            for j in range(1, SIDE):
                total += cheb[i, j] * cells[j]
            slopes[16 * i : 16 * i + 16, :] = total * scale_x
        spot = source * RING + x
        for what, src, dst in ((0, line, xc), (1, slopes, xx)):
            for mask in (2, 3) if rr == 0 else (1,):
                start_x(what, k, mask, src.at[half(partner[mask], 64)], dst.at[spot])
            if rr == 1:
                dst[spot] = src[half(x, 64), :]

    def pass_grad(k, source, rr, line):
        spot = source * RING + x
        for mask in (2, 3) if rr == 0 else (1,):
            start_x(2, k, mask, line.at[half(partner[mask], 32)], xy.at[spot, 1])
        if rr == 1:
            xy[spot, 1] = line[half(x, 32), :]

    for rr in range(2):
        at = pl.multiple_of(row_start(z, rr), 128)
        pass_values(0, z, rr, coeff.at[pl.ds(at, 128)])
        pass_grad(0, z, rr, grad_y.at[pl.ds(at + 64, 64)])

    zcopy[0, 1, 0].wait_recv()
    for rr in range(2):
        send_values(2, rr)
    ones = traits[0:NODES, :]
    weights = traits[NODES : 2 * NODES, :]
    node = lax.broadcasted_iota(jnp.int32, (NODES, 128), 0)
    stiffness = stiff[...]
    on_diag = lax.broadcasted_iota(jnp.int32, (NODES, NODES), 0) == lax.broadcasted_iota(
        jnp.int32, (NODES, NODES), 1
    )
    stiff_diag = jnp.sum(jnp.where(on_diag, stiffness, 0.0), axis=1, keepdims=True)
    stiff_high, stiff_low = split(stiffness)
    stiff_all = jnp.concatenate([stiff_high, stiff_high, stiff_low], axis=1)

    def spread(first, second):
        high, low = split(jnp.concatenate([first, second], axis=1))
        cells = jnp.concatenate([high, low, high], axis=0)
        both = jnp.dot(stiff_all, cells, preferred_element_type=F32)
        return both[:, :128], both[:, 128:]

    def local_terms(lumped, inverse, rates, scale, lam_to, diag_to):
        wall = jnp.where(node < SIDE, jnp.broadcast_to(rates, (NODES, 128)), 0.0)
        stiff_part = stiff_diag * scale
        for q in range(modes):
            wave = ((m * modes + q + 1) // 2).astype(F32) * (2.0 / (modes * RING * RING))
            value = (INV_STEP + (wave * wave) * inverse) * lumped + wall
            lam_to[q] = value
            diag_to[q] = stiff_part + value

    local_terms(ones, weights, flow, elem_scale, lam, rate)
    for q in range(modes):
        fld[q] = coeff[pl.ds(q, NODES, stride=modes), :]

    first_nodes = pl.ds(0, SIDE, stride=SIDE)
    last_nodes = pl.ds(SIDE - 1, SIDE, stride=SIDE)
    def turn(value, shift):
        return pltpu.roll(value, shift % 128, 1) if shift % 128 else value

    def join_rows(values, q):
        lower = values[q, 0:SIDE, :]
        upper = values[q, NODES - SIDE : NODES, :]
        values[q, 0:SIDE, :] = lower + jnp.where(row > 0, turn(upper, 1), 0.0)
        values[q, NODES - SIDE : NODES, :] = upper + jnp.where(row < 15, turn(lower, -1), 0.0)

    for pair in range(modes // 2):
        applied = spread(fld[2 * pair], fld[2 * pair + 1])
        for h in range(2):
            q = 2 * pair + h
            res[q] = (INV_STEP * ones - lam[q]) * fld[q] - elem_scale * applied[h]
    quad = lane // 32
    outer = col % 2

    def pack(pieces, send, shift):
        for g in range(len(pieces) // 4):
            total = None
            for k in range(4):
                piece = turn(pieces[4 * g + k], 32 * k + shift)
                total = piece if total is None else jnp.where(quad == k, piece, total)
            send[g] = total

    def join_inner(values):
        for q in range(modes):
            low, high = values[q, first_nodes, :], values[q, last_nodes, :]
            values[q, first_nodes, :] = low + jnp.where(col == 0, 0.0, turn(high, 16))
            values[q, last_nodes, :] = high + jnp.where(col == 7, 0.0, turn(low, -16))

    def join_halo(values, beside, inner, both):
        for g in range(modes // 4):
            left_low, left_high = beside[0, g, first_nodes, :], beside[0, g, last_nodes, :]
            right_low, right_high = beside[1, g, first_nodes, :], beside[1, g, last_nodes, :]
            add_left = turn(left_low, -16)
            add_right = turn(right_high, 16)
            for k in range(4):
                q = 4 * g + k
                low, high = values[q, first_nodes, :], values[q, last_nodes, :]
                near = turn(left_high, -32 * k - 16)
                past = turn(right_low, 112 - 32 * k)
                values[q, first_nodes, :] = jnp.where(col == 0, low + near, low)
                values[q, last_nodes, :] = jnp.where(col == 7, high + past, high)
                if both:
                    add_left = jnp.where(col == 2 * k + 1, turn(low, 32 * k + 16), add_left)
                    add_right = jnp.where(col == 2 * k, turn(high, 32 * k + 16), add_right)
            if both:
                if not inner:
                    add_left = jnp.where(outer == 1, add_left, 0.0)
                    add_right = jnp.where(outer == 0, add_right, 0.0)
                beside[0, g, last_nodes, :] = left_high + add_left
                beside[1, g, first_nodes, :] = right_low + add_right
                if inner:
                    beside[0, g, first_nodes, :] = left_low + jnp.where(
                        outer == 1, turn(left_high, 16), 0.0
                    )
                    beside[1, g, last_nodes, :] = right_high + jnp.where(
                        outer == 0, turn(right_low, -16), 0.0
                    )
        for q in range(modes):
            join_rows(values, q)
        if both:
            for side in range(2):
                for g in range(modes // 4):
                    join_rows(beside.at[side], g)

    for k, d in lots:
        source = (z - d + RING) % RING
        for rr in range(2):
            if rr == 0:
                zcopy[3, d, 0].wait_recv()
            if (d, rr) != (1, 0):
                zcopy[0, d, rr].wait_recv()
            line = zc.at[source, rows[rr]]
            line[112:128, :] = last_node(line[0:16, :], far_ends[source], rr)
            pass_values(k, source, rr, line)
        if k == 2:
            for mask in (1, 2, 3):
                xcopy[0, 0, mask].wait_recv()
                xcopy[0, 1, mask].wait_recv()
            send_first_pairs()
            for rr, d in waves[4:] + waves[:4]:
                at = pl.multiple_of(row_start((z + d) % RING, rr) + 64, 64)
                start_z(2, d, rr, grad_y.at[pl.ds(at, 48)], zg.at[z, rows[rr], pl.ds(0, 48)])

    settle(trait_copies, theirs)
    join_inner(rate)
    side_scale = []
    here = lane >= 64
    for side in range(2):
        def window(mine, others):
            return jnp.where(here == (side == 0), turn(mine, 64), turn(others, 64))

        local_terms(
            window(ones, theirs[side, 0:NODES, :]),
            window(weights, theirs[side, NODES : 2 * NODES, :]),
            window(flow, theirs[side, 2 * NODES + 1 : 2 * NODES + 2, :]),
            window(elem_scale, theirs[side, 2 * NODES : 2 * NODES + 1, :]),
            work,
            inc,
        )
        join_inner(inc)
        for q in range(modes):
            at = first_nodes if side == 0 else last_nodes
            value = turn(inc[q, at, :], 64)
            rate[q, at, :] = jnp.where(col == (0 if side == 0 else 7), value, rate[q, at, :])
            join_rows(inc, q)
            inc[q] = RELAX / inc[q]
        shift = -32 if side == 0 else -64
        pack([work[q] for q in range(modes)], side_lam.at[side], shift)
        pack([inc[q] for q in range(modes)], side_rate.at[side], shift)

        @pl.when(jnp.logical_not(has_left if side == 0 else has_right))
        def _():
            side_rate[side] = jnp.zeros(side_rate.shape[1:], F32)

        scales = window(elem_scale, theirs[side, 2 * NODES : 2 * NODES + 1, :])
        total = None
        for k in range(4):
            piece = turn(scales, 32 * k + shift)
            total = piece if total is None else jnp.where(quad == k, piece, total)
        side_scale.append(total)
    for q in range(modes):
        join_rows(rate, q)
        rate[q] = RELAX / rate[q]

    bcopy = []
    for part in range(2):
        which_pair = (part + 1 + x % 2) % 2
        for k, d in lots if part == 1 else ():
            source = (z - d + RING) % RING
            for rr in range(2):
                zcopy[2, d, rr].wait_recv()
                line = zg.at[source, rows[rr]]
                line[48:64, :] = last_node(line[0:16, :], far_ends[source], 2 + rr)
                pass_grad(k, source, rr, line)
        if part == 0:
            for copy in later[6:]:
                copy.wait()
        if part == 0:
            for (what, k, mask), copy in xcopy.items():
                if what < 2 and (what, k) not in ((0, 0), (0, 1)):
                    copy.wait_recv()

        def advection(kind, src):
            pieces = []
            for h in range(2):
                at = pl.ds(pl.multiple_of(32 * which_pair + 16 * h, 16), 16)
                piece = src[:, part, 16 * h : 16 * h + 16, :] if kind == 1 else src[:, at, :]
                pieces.append(piece.reshape(-1, 128))
            which = 0 if kind == 0 else 2
            phys = dot3(tab[which], tab[which + 1], jnp.concatenate(pieces, axis=1))
            speed = jnp.concatenate(
                [vel[kind, 2 * which_pair], vel[kind, 2 * which_pair + 1]], axis=1
            )
            return speed.astype(F32) * phys

        partial[...] = advection(0, xc) + advection(2, xx)
        if part == 0:
            for copy in gcopy:
                copy.wait_recv()
        else:
            for (what, k, mask), copy in xcopy.items():
                if what == 2:
                    copy.wait_recv()
        advect = partial[...] + advection(1, xy)
        back = dot3(tab[4], tab[5], advect)
        for h in range(2):
            for t in range(RING * RING):
                hat[part, t, 16 * h : 16 * h + 16, :] = back[
                    16 * t : 16 * t + 16, 128 * h : 128 * h + 128
                ]
        mine = pl.ds(pl.multiple_of(m * 64 + 32 * which_pair, 32), 32)
        for d, (dz, dx) in enumerate(order, 1):
            target = (z + dz) % RING * RING + (x + dx) % RING
            copy = pltpu.make_async_remote_copy(
                src_ref=hat.at[part, target],
                dst_ref=adv.at[mine],
                send_sem=bs.at[part, d - 1],
                recv_sem=br.at[part, d - 1],
                device_id={"mode": target},
                device_id_type=MESH,
            )
            copy.start()
            bcopy.append(copy)
        adv[mine, :] = hat[part, m]
    for copy in bcopy:
        copy.wait_recv()

    for q in range(modes):
        res[q] = res[q] - ones * adv[pl.ds(q, NODES, stride=modes), :]
    join_inner(res)
    for side in range(2):
        pack([res[q] for q in range(modes)], tsend.at[side], 32 * side)
    settle(swap([(tsend.at[0], halo.at[1]), (tsend.at[1], halo.at[0])], 1), halo)
    join_halo(res, halo, False, True)

    for q in range(modes):
        inc[q] = rate[q] * res[q]
    for side in range(2):
        for g in range(modes // 4):
            far[side, g] = side_rate[side, g] * halo[side, g]
    for sweep in range(1, SWEEPS):
        for pair in range(modes // 2):
            applied = spread(inc[2 * pair], inc[2 * pair + 1])
            for h in range(2):
                q = 2 * pair + h
                work[q] = elem_scale * applied[h] + lam[q] * inc[q]
        for side in range(2):
            for pair in range(modes // 8):
                applied = spread(far[side, 2 * pair], far[side, 2 * pair + 1])
                for h in range(2):
                    g = 2 * pair + h
                    beside[side, g] = side_scale[side] * applied[h] + side_lam[side, g] * far[side, g]
        join_inner(work)
        join_halo(work, beside, True, sweep < SWEEPS - 1)
        for q in range(modes):
            total = inc[q] + rate[q] * (res[q] - work[q])
            if sweep < SWEEPS - 1:
                inc[q] = total
            else:
                out[pl.ds(q, NODES, stride=modes), :] = fld[q] + total
        if sweep < SWEEPS - 1:
            for side in range(2):
                for g in range(modes // 4):
                    far[side, g] = far[side, g] + side_rate[side, g] * (
                        halo[side, g] - beside[side, g]
                    )

    for copies in (zcopy, xcopy):
        for copy in copies.values():
            copy.wait_send()
    for copy in gcopy + bcopy:
        copy.wait_send()


def local(
    tables, coeff, vel_axial, vel_radial, swirl_rate, col_width, row_height, stiffness, stiff_elem,
    mass, azim_weight, wall_flag, transfer,
):
    modes = coeff.shape[1]
    planes = vel_axial.shape[1]
    dma = pltpu.SemaphoreType.DMA
    field = pltpu.VMEM((modes, NODES, 128), F32)
    flat = pltpu.VMEM((NODES * modes, 128), F32)
    columns = pltpu.VMEM((2, modes // 4, NODES, 128), F32)
    rows = pltpu.VMEM((RING, 2, 8 * modes, 128), F32)
    blocks = pltpu.VMEM((RING * RING, 4 * modes, 128), F32)
    halves = pltpu.VMEM((RING * RING, 2, 2 * modes, 128), F32)
    operands = (
        coeff.reshape(NODES * modes, 128),
        swirl_rate,
        vel_radial,
        vel_axial,
        jnp.asarray(tables),
        col_width,
        row_height,
        stiffness,
        stiff_elem.reshape(1, 128),
        mass,
        azim_weight,
        wall_flag,
        transfer,
    )
    result = pl.pallas_call(
        functools.partial(kernel, modes),
        out_shape=pltpu.VMEM((NODES * modes, 128), F32),
        in_specs=[pl.BlockSpec(memory_space=pl.ANY)] * len(operands),
        out_specs=pl.BlockSpec(memory_space=pltpu.VMEM),
        scratch_shapes=[
            flat,
            pltpu.SMEM(col_width.shape, F32),
            pltpu.SMEM(row_height.shape, F32),
            pltpu.VMEM((NODES, NODES), F32),
            pltpu.VMEM((1, 128), F32),
            pltpu.VMEM((2 * NODES + SIDE, 128), F32),
            pltpu.SMEM(wall_flag.shape, jnp.int32),
            pltpu.SMEM(transfer.shape, F32),
            pltpu.VMEM((3, 4, planes, 128), BF16),
            pltpu.VMEM(tables.shape, BF16),
            flat,
            pltpu.VMEM((RING * modes, 128), F32),
            pltpu.VMEM((RING, modes, 128), F32),
            rows,
            pltpu.VMEM((RING, 2, 4 * modes, 128), F32),
            rows,
            blocks,
            blocks,
            halves,
            pltpu.VMEM((planes, 256), F32),
            pltpu.VMEM((2, RING * RING, 2 * modes, 128), F32),
            flat,
            field,
            field,
            field,
            field,
            field,
            field,
            pltpu.VMEM((2, 2 * NODES + SIDE, 128), F32),
            columns,
            columns,
            columns,
            columns,
            columns,
            columns,
            dma((13,)),
            dma((4, 3, 2)),
            dma((4, 3, 2)),
            dma((3, 4, 3)),
            dma((3, 4, 3)),
            dma((15,)),
            dma((15,)),
            dma((2, 15)),
            dma((2, 15)),
            dma((2, 2)),
            dma((2, 2)),
        ],
        compiler_params=pltpu.CompilerParams(collective_id=0, has_side_effects=True),
    )(*operands)
    return result.reshape(coeff.shape)


def solution(mesh):
    tables = fourier_tables(256)
    return jax.shard_map(
        functools.partial(local, tables),
        mesh=mesh,
        in_specs=(
            P(None, "mode", "elem"),
            P("mode", None, "elem"),
            P("mode", None, "elem"),
            P("mode", None, "elem"),
            P("elem"),
            P(),
            P(),
            P("elem"),
            P(None, "elem"),
            P(None, "elem"),
            P("elem"),
            P("elem"),
        ),
        out_specs=P(None, "mode", "elem"),
        check_vma=False,
    )
```
